512 devices in a mesh: tx: 16 (over z, core), ty: 8 (over y_hi, x), mode: 4 (over y_lo).
Axes of the slice: x: 4, y: 8 (y_hi: 2, y_lo: 4; y = y_hi * 4 + y_lo), z: 8, core: 2. Of those that a mesh axis runs over, the one named last changes fastest.
Arguments:
- object_field: float32 [2, 2048, 2048], P(None, 'tx', 'ty'), may hold values from -5 to 5
- probe: float32 [2, 8, 256, 256], P(None, 'mode'), may hold values from -1.5 to 1.5
- amplitudes: bfloat16 [16, 8, 2, 256, 256], P('tx', 'ty'), may hold values from 0.29882812 to 2.5
- centers: int32 [16, 8, 2, 2], P('tx', 'ty'), may hold values from 0 to 255, as said below
- live: int32 [16, 8], P('tx', 'ty'), may hold values from 1 to 2, as said below
Outputs:
- updated: float32 [2, 2048, 2048], P(None, 'tx', 'ty')
The draws below stay inside these ranges and needn't reach their ends.
Inputs may be any that keep to these rules, and one draw needn't show every extreme that they name: `centers`: the first component is under 128, the second under 256; some live slot sits at offsets (127, 255) and some at (0, 0). A tile's positions fill its slots 0 to live - 1; some tile has all 2 slots live and some only one.
All inputs are finite; a program needn't handle non-finite values.
Results may differ from the reference program's by a relative error of at most 0.006.
Values may be sent and summed in bfloat16 or wider, within the bound.
A program may use at most 64 MiB of HBM per device.

```python
import math
import jax
import jax.numpy as jnp
from jax import lax

W = 256
MODES = 8
SLOTS = 2
TR = 128
TC = 256
NTR = 16
NTC = 8
NX = 2048
NY = 2048


def draw_centers(key, part):
    key_spots = jax.random.fold_in(key, 11)
    key_high = jax.random.fold_in(key, 12)
    key_low = jax.random.fold_in(key, 13)
    limits = jnp.array([TR, TC], dtype=jnp.int32)
    spots = jax.random.randint(key_spots, (NTR * NTC, SLOTS, 2), 0, limits)
    high_tile = jax.random.randint(key_high, (), 0, NTR * NTC)
    low_tile = (high_tile + 1 + jax.random.randint(key_low, (), 0, NTR * NTC - 1)) % (NTR * NTC)
    spots = spots.at[high_tile, 0].set(limits - 1)
    spots = spots.at[low_tile, 0].set(jnp.zeros((2,), jnp.int32))
    return spots.reshape(NTR, NTC, SLOTS, 2)


def draw_live(key, part):
    key_base = jax.random.fold_in(key, 21)
    key_full = jax.random.fold_in(key, 22)
    key_most = jax.random.fold_in(key, 23)
    key_least = jax.random.fold_in(key, 24)
    tiles = NTR * NTC
    base = 1 + jax.random.randint(key_base, (tiles,), 0, max(1, SLOTS // 2))
    crowded = jax.random.randint(key_full, (tiles,), 0, 8) == 0
    counts = jnp.where(crowded, SLOTS, base).astype(jnp.int32)
    most_tile = jax.random.randint(key_most, (), 0, tiles)
    least_tile = (most_tile + 1 + jax.random.randint(key_least, (), 0, tiles - 1)) % tiles
    counts = counts.at[most_tile].set(SLOTS)
    counts = counts.at[least_tile].set(1)
    return counts.reshape(NTR, NTC)


def steps_of(key, shape, shards, least, largest):
    gain, own = 1.0, jax.random.fold_in(key, 6)
    for axis_at, shards_of in shards:
        heights = jnp.exp(jax.random.uniform(jax.random.fold_in(own, axis_at), (shards_of,), jnp.float32, least / len(shards), largest / len(shards)))
        gain = gain * jnp.repeat(heights, shape[axis_at] // shards_of).reshape([-1 if axis == axis_at else 1 for axis in range(len(shape))])
    return gain


def noise(rng, dims, spread, reach, cuts=(), held_as=jnp.bfloat16):
    result = spread * jax.random.normal(rng, dims, jnp.float32)
    if cuts:
        result = result * steps_of(rng, dims, cuts, -0.22, 0.18)
    return jnp.clip(result, -reach, reach).astype(held_as)


def setup_inputs(seed: int = 0) -> dict:
    arg_keys = jax.random.split(jax.random.key(seed), 6)
    return {
        "object_field": noise(arg_keys[0], (2, NX, NY), 0.7, 5.0, ((1, 16), (2, 8)), jnp.float32),
        "probe": noise(arg_keys[1], (2, MODES, W, W), 0.25, 1.5, ((1, 4),), jnp.float32),
        "amplitudes": jnp.clip(0.29882812 + 2.2011719 * jax.random.uniform(arg_keys[2], (NTR, NTC, SLOTS, W, W), jnp.float32) ** steps_of(arg_keys[2], (NTR, NTC, SLOTS, W, W), ((0, 16), (1, 8)), -0.2, 0.2), 0.29882812, 2.5).astype(jnp.bfloat16),
        "centers": draw_centers(jax.random.fold_in(arg_keys[5], 71), 0),
        "live": draw_live(jax.random.fold_in(arg_keys[5], 71), 0),
    }


power_floor = 0.01
regularizer = 0.1

def dft_tables(pattern_side):
    index_line = jnp.arange(pattern_side, dtype=jnp.int32)
    product_table = index_line[:, None] * index_line[None, :] % pattern_side
    angle_table = product_table.astype(jnp.float32) * (2.0 * math.pi / pattern_side)
    scaling = 1.0 / math.sqrt(pattern_side)
    table_real = (jnp.cos(angle_table) * scaling).astype(jnp.bfloat16)
    table_imaginary = (-jnp.sin(angle_table) * scaling).astype(jnp.bfloat16)
    return (table_real, table_imaginary)

def left_mult(matrix, signal):
    return jnp.einsum('uv,kvw->kuw', matrix.astype(jnp.float32), signal.astype(jnp.float32))

def right_mult(signal, matrix):
    return jnp.einsum('kuv,vw->kuw', signal.astype(jnp.float32), matrix.astype(jnp.float32))

def left_apply(matrix_real, matrix_imaginary, signal_real, signal_imaginary):
    return (left_mult(matrix_real, signal_real) - left_mult(matrix_imaginary, signal_imaginary), left_mult(matrix_real, signal_imaginary) + left_mult(matrix_imaginary, signal_real))

def right_apply(matrix_real, matrix_imaginary, signal_real, signal_imaginary):
    return (right_mult(signal_real, matrix_real) - right_mult(signal_imaginary, matrix_imaginary), right_mult(signal_real, matrix_imaginary) + right_mult(signal_imaginary, matrix_real))

def slot_gradient(patch, amplitude, probe_real, probe_imaginary, table_real, table_imaginary):
    patch_real = patch[0].astype(jnp.float32)
    patch_imaginary = patch[1].astype(jnp.float32)
    exit_real = (probe_real * patch_real - probe_imaginary * patch_imaginary).astype(jnp.bfloat16)
    exit_imaginary = (probe_real * patch_imaginary + probe_imaginary * patch_real).astype(jnp.bfloat16)
    half_real, half_imaginary = left_apply(table_real, table_imaginary, exit_real, exit_imaginary)
    far_real, far_imaginary = right_apply(table_real, table_imaginary, half_real.astype(jnp.bfloat16), half_imaginary.astype(jnp.bfloat16))
    power = lax.optimization_barrier(jnp.sum(far_real * far_real + far_imaginary * far_imaginary, axis=0))
    factor = amplitude.astype(jnp.float32) / jnp.sqrt(power + power_floor)
    fixed_real = (far_real * factor).astype(jnp.bfloat16)
    fixed_imaginary = (far_imaginary * factor).astype(jnp.bfloat16)
    back_half_real, back_half_imaginary = left_apply(table_real, -table_imaginary, fixed_real, fixed_imaginary)
    back_real, back_imaginary = right_apply(table_real, -table_imaginary, back_half_real.astype(jnp.bfloat16), back_half_imaginary.astype(jnp.bfloat16))
    diff_real = back_real - exit_real.astype(jnp.float32)
    diff_imaginary = back_imaginary - exit_imaginary.astype(jnp.float32)
    grad_real = lax.optimization_barrier(jnp.sum(probe_real * diff_real + probe_imaginary * diff_imaginary, axis=0))
    grad_imaginary = lax.optimization_barrier(jnp.sum(probe_real * diff_imaginary - probe_imaginary * diff_real, axis=0))
    return (grad_real, grad_imaginary)

def reference(object_field, probe, amplitudes, centers, live):
    half_width = W // 2
    table_real, table_imaginary = dft_tables(W)
    object_low = object_field.astype(jnp.bfloat16)
    padded = jnp.pad(object_low, ((0, 0), (half_width, half_width), (half_width, half_width)))
    probe_real = probe[0]
    probe_imaginary = probe[1]
    probe_power = lax.optimization_barrier(jnp.sum(probe_real * probe_real + probe_imaginary * probe_imaginary, axis=0))
    total_items = NTR * NTC * SLOTS
    item_index = jnp.arange(total_items, dtype=jnp.int32)
    tile_index = item_index // SLOTS
    slot_index = item_index % SLOTS
    tile_row = tile_index // NTC
    tile_col = tile_index % NTC
    flat_centers = centers.reshape(total_items, 2).astype(jnp.int32)
    flat_live = live.reshape(NTR * NTC).astype(jnp.int32)
    live_flag = slot_index < flat_live[tile_index]
    row_start = (tile_row * TR + flat_centers[:, 0]).astype(jnp.int32)
    col_start = (tile_col * TC + flat_centers[:, 1]).astype(jnp.int32)
    flat_amplitudes = amplitudes.reshape(total_items, W, W)
    anchor = jnp.zeros((), jnp.int32)
    summed = jnp.zeros((3, NX + W, NY + W), jnp.float32)

    def advance(summed, record):
        row_at, col_at, amplitude, flag = record

        def work(summed):
            patch = lax.dynamic_slice(padded, (anchor, row_at, col_at), (2, W, W))
            grad_real, grad_imaginary = slot_gradient(patch, amplitude, probe_real, probe_imaginary, table_real, table_imaginary)
            block = jnp.stack([grad_real, grad_imaginary, probe_power])
            current = lax.dynamic_slice(summed, (anchor, row_at, col_at), (3, W, W))
            return lax.dynamic_update_slice(summed, current + block, (anchor, row_at, col_at))
        return (lax.cond(flag, work, lambda keep: keep, summed), None)
    summed, _ = lax.scan(advance, summed, (row_start, col_start, flat_amplitudes, live_flag))
    inner = summed[:, half_width:half_width + NX, half_width:half_width + NY]
    return object_field + inner[:2] / (inner[2] + regularizer)
```

```python
import math

import jax
import jax.numpy as jnp
import numpy as np
from jax import lax
from jax.experimental import pallas as pl
from jax.experimental.pallas import tpu as pltpu
from jax.sharding import PartitionSpec as P

power_floor = 0.01
regularizer = 0.1
W = 256
HW = 128
TR = 128
TC = 256
Q = 32
f32 = jnp.float32
bf16 = jnp.bfloat16
i32 = jnp.int32
MESH = pl.DeviceIdType.MESH


def dft_tables():
    line = np.arange(W)
    angle = ((line[:, None] * line[None, :]) % W).astype(np.float32) * np.float32(2.0 * math.pi / W)
    scaling = np.float32(1.0 / math.sqrt(W))
    return jnp.asarray(
        np.stack([np.cos(angle) * scaling, -np.sin(angle) * scaling]).astype(np.float32)
    ).astype(bf16)


def dot(a, b):
    return jnp.dot(a, b, preferred_element_type=f32)


def one_hot(cond):
    return jnp.where(cond, 1.0, 0.0).astype(bf16)


def iota(shape, dim):
    return lax.broadcasted_iota(i32, shape, dim)


def kernel(
    obj_hbm,
    probe_hbm,
    amp_hbm,
    table_hbm,
    centers_ref,
    live_ref,
    out_ref,
    obj_v,
    probe_v,
    amp_v,
    tab,
    pb,
    pad,
    ib,
    mat_a,
    mat_b,
    mat_bc,
    mat_d,
    sel_p,
    sel_s,
    sel_pt,
    sel_st,
    patch,
    x_s,
    h_s,
    far_s,
    pow_s,
    wt,
    fix_s,
    r_s,
    back_s,
    grad,
    ext,
    zrecv,
    xsend,
    xrecv,
    mid,
    core_s,
    rs_s,
    rs_r,
    ag_s,
    wq,
    local_sem,
    send,
    recv,
):
    tx, ty, m = lax.axis_index("tx"), lax.axis_index("ty"), lax.axis_index("mode")
    nx, ny, nm = lax.axis_size("tx"), lax.axis_size("ty"), lax.axis_size("mode")
    half_ny = ny // 2
    c = lax.rem(tx, 2)
    slot = m // 2
    part = lax.rem(m, 2)

    def at(tx_at, ty_at, m_at):
        return (tx_at, ty_at, m_at)

    right_ty = lax.rem(ty + 1, ny)
    left_ty = lax.rem(ty + ny - 1, ny)
    right_m = jnp.where(lax.rem(ty, half_ny) == half_ny - 1, nm - 1 - m, m)
    left_m = jnp.where(lax.rem(ty, half_ny) == 0, nm - 1 - m, m)
    right = at(tx, right_ty, right_m)
    left = at(tx, left_ty, left_m)
    up = at(lax.rem(tx + nx - 1, nx), ty, m)
    down = at(lax.rem(tx + 1, nx), ty, m)
    partner = at(tx + 1 - 2 * c, ty, m)
    far_ty = lax.rem(ty + half_ny, ny)
    ring_up = at(tx, jnp.where(m == nm - 1, far_ty, ty), lax.rem(m + 1, nm))
    ring_down = at(tx, jnp.where(m == 0, far_ty, ty), lax.rem(m + nm - 1, nm))
    mates = [at(tx, ty, lax.rem(m + d, nm)) for d in (1, 2, 3)]

    def remote(index, src, dst, to):
        return pltpu.make_async_remote_copy(
            src_ref=src,
            dst_ref=dst,
            send_sem=send.at[index],
            recv_sem=recv.at[index],
            device_id=to,
            device_id_type=MESH,
        )

    started = []

    def go(index, src, dst, to):
        copy = remote(index, src, dst, to)
        copy.start()
        started.append(copy)
        return copy

    loads = [
        pltpu.make_async_copy(obj_hbm, obj_v, local_sem.at[0]),
        pltpu.make_async_copy(probe_hbm, probe_v, local_sem.at[1]),
        pltpu.make_async_copy(table_hbm, tab, local_sem.at[2]),
        pltpu.make_async_copy(amp_hbm.at[0, 0], amp_v, local_sem.at[3]),
    ]
    for load in loads:
        load.start()

    barrier = pltpu.get_barrier_semaphore()
    meets = [left, right, up, down, ring_up, ring_down, *mates]
    for to in meets:
        pl.semaphore_signal(barrier, inc=1, device_id=to, device_id_type=MESH)

    row = iota((8, 128), 0)
    ints = jnp.zeros((8, 128), i32)
    for at_row, value in enumerate(
        [
            centers_ref[0, 0, 0, 0],
            centers_ref[0, 0, 0, 1],
            centers_ref[0, 0, 1, 0],
            centers_ref[0, 0, 1, 1],
            live_ref[0, 0],
        ]
    ):
        ints = jnp.where(row == at_row, value, ints)
    ib[1, 1] = ints

    loads[0].wait()
    for p in range(2):
        pad[p, HW : HW + TR, HW : HW + TC] = obj_v[p].astype(bf16)
    pl.semaphore_wait(barrier, len(meets))

    mid_rows = pl.ds(HW, TR)
    top_rows = pl.ds(0, HW)
    low_rows = pl.ds(HW + TR, HW)
    mid_cols = pl.ds(HW, TC)
    left_cols = pl.ds(0, HW)
    right_cols = pl.ds(HW + TC, HW)
    to_left = go(0, pad.at[:, mid_rows, pl.ds(HW, HW)], pad.at[:, mid_rows, right_cols], left)
    to_right = go(1, pad.at[:, mid_rows, pl.ds(TC, HW)], pad.at[:, mid_rows, left_cols], right)
    ints_left = go(2, ib.at[1, 1], ib.at[1, 2], left)
    ints_right = go(3, ib.at[1, 1], ib.at[1, 0], right)
    z_up = go(4, pad.at[:, mid_rows, mid_cols], pad.at[:, low_rows, mid_cols], up)
    z_down = go(5, pad.at[:, mid_rows, mid_cols], pad.at[:, top_rows, mid_cols], down)

    loads[1].wait()
    for p in range(2):
        pb[0, 0, p] = probe_v[p, c].astype(bf16)
    ring = {}
    ring[3, 0] = go(12, pb.at[0, 0, 0], pb.at[3, 0, 0], ring_up)
    ring[1, 1] = go(13, pb.at[0, 0, 1], pb.at[1, 0, 1], ring_down)
    ring[3, 1] = go(14, pb.at[0, 0, 1], pb.at[3, 0, 1], ring_up)
    ring[1, 0] = go(15, pb.at[0, 0, 0], pb.at[1, 0, 0], ring_down)
    for p in range(2):
        pb[0, 1, p] = probe_v[p, 1 - c].astype(bf16)

    loads[2].wait()
    fr, fi = tab[0], tab[1]
    rows_here = pl.ds(pl.multiple_of(part * HW, HW), HW)
    fr_half, fi_half = tab[0, rows_here, :], tab[1, rows_here, :]
    mat_a[0:HW, 0:W] = fr_half
    mat_a[0:HW, W : 2 * W] = -fi_half
    mat_a[HW:W, 0:W] = fi_half
    mat_a[HW:W, W : 2 * W] = fr_half
    mat_b[0:W, 0:W] = fr
    mat_b[0:W, W : 2 * W] = fi
    mat_b[W : 2 * W, 0:W] = -fi
    mat_b[W : 2 * W, W : 2 * W] = fr
    mat_bc[0:W, 0:W] = fr
    mat_bc[0:W, W : 2 * W] = -fi
    mat_bc[W : 2 * W, 0:W] = fi
    mat_bc[W : 2 * W, W : 2 * W] = fr
    cols_here = pl.ds(pl.multiple_of(part * HW, HW), HW)
    fr_cols, fi_cols = tab[0, :, cols_here], tab[1, :, cols_here]
    mat_d[0:W, 0:HW] = fr_cols
    mat_d[0:W, HW:W] = fi_cols
    mat_d[W : 2 * W, 0:HW] = -fi_cols
    mat_d[W : 2 * W, HW:W] = fr_cols

    row_at = jnp.where(slot == 0, centers_ref[0, 0, 0, 0], centers_ref[0, 0, 1, 0])
    col_at = jnp.where(slot == 0, centers_ref[0, 0, 0, 1], centers_ref[0, 0, 1, 1])
    row_from = jnp.where(tx == 0, HW, 0)
    row_to = jnp.where(tx == nx - 1, HW + TR, TR + W)
    col_from = jnp.where(ty == 0, HW, 0)
    col_to = jnp.where(ty == ny - 1, HW + TC, TC + W)

    def selection(shape, outer, base, start, stop):
        big, small = iota(shape, outer), iota(shape, 1 - outer)
        return one_hot((big == small + base) & (big >= start) & (big < stop))

    sel_p[...] = selection((W, TR + W), 1, row_at, row_from, row_to)
    sel_pt[...] = selection((TR + W, W), 0, row_at, row_from, row_to)
    sel_s[...] = selection((TC + W, W), 0, col_at, col_from, col_to)
    sel_st[...] = selection((W, TC + W), 1, col_at, col_from, col_to)

    side = {}

    def pass_on(index, d, p):
        side[d, p] = go(index, pb.at[d, 0, p], pb.at[d, 1, p], partner)

    ring[3, 0].wait_recv()
    ring[2, 0] = go(16, pb.at[3, 0, 0], pb.at[2, 0, 0], ring_up)
    ring[1, 1].wait_recv()
    ring[2, 1] = go(17, pb.at[1, 0, 1], pb.at[2, 0, 1], ring_down)
    pass_on(18, 3, 0)
    pass_on(19, 1, 1)

    to_left.wait_recv()
    to_right.wait_recv()
    z_sides = [
        go(6, pad.at[:, mid_rows, left_cols], pad.at[:, low_rows, left_cols], up),
        go(7, pad.at[:, mid_rows, right_cols], pad.at[:, low_rows, right_cols], up),
        go(8, pad.at[:, mid_rows, left_cols], pad.at[:, top_rows, left_cols], down),
        go(9, pad.at[:, mid_rows, right_cols], pad.at[:, top_rows, right_cols], down),
    ]
    ints_left.wait_recv()
    ints_right.wait_recv()
    ints_up = go(10, ib.at[1], ib.at[2], up)
    ints_down = go(11, ib.at[1], ib.at[0], down)

    ring[3, 1].wait_recv()
    pass_on(20, 3, 1)
    ring[1, 0].wait_recv()
    pass_on(21, 1, 0)

    z_up.wait_recv()
    z_down.wait_recv()
    for copy in z_sides:
        copy.wait_recv()
    for p in range(2):
        shifted = dot(sel_p[...], pad[p]).astype(bf16)
        patch[p] = dot(shifted, sel_s[...])

    ring[2, 0].wait_recv()
    pass_on(22, 2, 0)
    ring[2, 1].wait_recv()
    pass_on(23, 2, 1)

    chunk = 32

    def forward(d, first):
        def exits(i, carry):
            at_rows = pl.ds(pl.multiple_of(i * chunk, chunk), chunk)
            low_rows_at = pl.ds(pl.multiple_of(W + i * chunk, chunk), chunk)
            o_r, o_i = patch[0, at_rows, :], patch[1, at_rows, :]
            weight = jnp.zeros((chunk, W), f32) if first else wt[at_rows, :]
            for j in range(2):
                p_r = pb[d, j, 0, at_rows, :].astype(f32)
                p_i = pb[d, j, 1, at_rows, :].astype(f32)
                x_s[j, at_rows, :] = (p_r * o_r - p_i * o_i).astype(bf16)
                x_s[j, low_rows_at, :] = (p_r * o_i + p_i * o_r).astype(bf16)
                weight = weight + (p_r * p_r + p_i * p_i)
            wt[at_rows, :] = weight
            return carry

        lax.fori_loop(0, W // chunk, exits, 0)
        for j in range(2):
            half = dot(mat_a[...], x_s[j]).astype(bf16)
            h_s[j * HW : (j + 1) * HW, 0:W] = half[0:HW]
            h_s[j * HW : (j + 1) * HW, W : 2 * W] = half[HW:W]
        far_s[d] = dot(h_s[...], mat_b[...])

        def powers(i, carry):
            at_rows = pl.ds(pl.multiple_of(i * chunk, chunk), chunk)
            next_rows = pl.ds(pl.multiple_of(HW + i * chunk, chunk), chunk)
            total = jnp.zeros((chunk, W), f32) if first else pow_s[at_rows, :]
            for rows in (at_rows, next_rows):
                a, b = far_s[d, rows, 0:W], far_s[d, rows, W : 2 * W]
                total = total + (a * a + b * b)
            pow_s[at_rows, :] = total
            return carry

        lax.fori_loop(0, HW // chunk, powers, 0)

    forward(0, True)
    side[3, 0].wait_recv()
    side[3, 1].wait_recv()
    forward(3, False)
    side[1, 1].wait_recv()
    side[1, 0].wait_recv()
    forward(1, False)
    side[2, 0].wait_recv()
    side[2, 1].wait_recv()
    forward(2, False)

    loads[3].wait()
    amplitude = amp_v[slot, rows_here, :].astype(f32)
    pow_s[...] = amplitude / jnp.sqrt(pow_s[...] + power_floor)

    def backward(d, carry):
        def fixes(i, carry):
            at_rows = pl.ds(pl.multiple_of(i * chunk, chunk), chunk)
            next_rows = pl.ds(pl.multiple_of(HW + i * chunk, chunk), chunk)
            factor = pow_s[at_rows, :]
            for rows in (at_rows, next_rows):
                fix_s[rows, 0:W] = (far_s[d, rows, 0:W] * factor).astype(bf16)
                fix_s[rows, W : 2 * W] = (far_s[d, rows, W : 2 * W] * factor).astype(bf16)
            return carry

        lax.fori_loop(0, HW // chunk, fixes, 0)
        half = dot(fix_s[...], mat_bc[...]).astype(bf16)
        for j in range(2):
            r_s[j, 0:HW, :] = half[j * HW : (j + 1) * HW, 0:W]
            r_s[j, HW:W, :] = half[j * HW : (j + 1) * HW, W : 2 * W]
        for j in range(2):
            back_s[j] = dot(mat_d[...], r_s[j])

        def grads(i, carry):
            at_rows = pl.ds(pl.multiple_of(i * chunk, chunk), chunk)
            low_rows_at = pl.ds(pl.multiple_of(W + i * chunk, chunk), chunk)
            g_r, g_i = grad[0, at_rows, :], grad[1, at_rows, :]
            for j in range(2):
                p_r = pb[d, j, 0, at_rows, :].astype(f32)
                p_i = pb[d, j, 1, at_rows, :].astype(f32)
                b_r, b_i = back_s[j, at_rows, :], back_s[j, low_rows_at, :]
                g_r = g_r + (p_r * b_r + p_i * b_i)
                g_i = g_i + (p_r * b_i - p_i * b_r)
            grad[0, at_rows, :] = g_r
            grad[1, at_rows, :] = g_i
            return carry

        lax.fori_loop(0, W // chunk, grads, 0)
        return carry

    for p in range(2):
        grad[p] = -0.5 * wt[...] * patch[p]
    lax.fori_loop(0, 4, backward, 0)

    counts = slot < live_ref[0, 0]
    for p in range(2):
        low = jnp.where(counts, grad[p], 0.0).astype(bf16)
        wide = dot(low, sel_st[...]).astype(bf16)
        ext[p] = dot(sel_pt[...], wide).astype(bf16)

    fold_up = go(24, ext.at[:, top_rows, :], zrecv.at[0], up)
    fold_down = go(25, ext.at[:, low_rows, :], zrecv.at[1], down)

    ints_up.wait_recv()
    ints_down.wait_recv()
    total = jnp.zeros((Q, TC), f32)
    low_weight = wt[...].astype(bf16)
    for a in range(3):
        for b in range(3):
            inside = (
                jnp.where(tx + (a - 1) >= 0, 1, 0)
                * jnp.where(tx + (a - 1) < nx, 1, 0)
                * jnp.where(ty + (b - 1) >= 0, 1, 0)
                * jnp.where(ty + (b - 1) < ny, 1, 0)
            )
            block = ib[a, b]
            alive = block[4:5, 0:1] * inside
            for s in range(2):
                row_of = m * Q + HW - HW * (a - 1) - block[2 * s : 2 * s + 1, 0:1]
                col_of = HW - TC * (b - 1) - block[2 * s + 1 : 2 * s + 2, 0:1]
                pick = one_hot(
                    (iota((Q, W), 1) == iota((Q, W), 0) + row_of) & (alive > s)
                )
                place = one_hot(iota((W, TC), 0) == iota((W, TC), 1) + col_of)
                picked = dot(pick, low_weight).astype(bf16)
                total = total + dot(picked, place)
    wq[...] = total

    fold_up.wait_recv()
    fold_down.wait_recv()
    for p in range(2):
        mid[p] = (
            ext[p, HW : HW + TR, :].astype(f32)
            + zrecv[0, p].astype(f32)
            + zrecv[1, p].astype(f32)
        )
        xsend[0, p] = mid[p, :, 0:HW].astype(bf16)
        xsend[1, p] = mid[p, :, HW + TC :].astype(bf16)
    cols_left = go(26, xsend.at[0], xrecv.at[1], left)
    cols_right = go(27, xsend.at[1], xrecv.at[0], right)
    cols_left.wait_recv()
    cols_right.wait_recv()
    for q in range(4):
        rows = slice(q * Q, (q + 1) * Q)
        for p in range(2):
            core_s[q, p, :, 0:HW] = mid[p, rows, HW : 2 * HW] + xrecv[0, p, rows, :].astype(f32)
            core_s[q, p, :, HW:TC] = mid[p, rows, 2 * HW : 3 * HW] + xrecv[1, p, rows, :].astype(f32)
            rs_s[q, p] = core_s[q, p].astype(bf16)
    sums = []
    for d in (1, 2, 3):
        sums.append(go(27 + d, rs_s.at[lax.rem(m + d, nm)], rs_r.at[d - 1], mates[d - 1]))
    total = core_s[m]
    for d in (1, 2, 3):
        sums[d - 1].wait_recv()
        total = total + rs_r[d - 1].astype(f32)
    scale = wq[...] + regularizer
    for p in range(2):
        ag_s[m, p] = (total[p] / scale).astype(bf16)
    gathers = [go(30 + d, ag_s.at[m], ag_s.at[m], mates[d - 1]) for d in (1, 2, 3)]
    for d in (1, 2, 3):
        gathers[d - 1].wait_recv()
    for q in range(4):
        for p in range(2):
            out_ref[p, q * Q : (q + 1) * Q, :] = ag_s[q, p]
    for copy in started:
        copy.wait_send()


def on_device(object_field, probe, amplitudes, centers, live):
    any_space = pl.BlockSpec(memory_space=pl.ANY)
    smem = pl.BlockSpec(memory_space=pltpu.SMEM)
    vmem = pltpu.VMEM
    update = pl.pallas_call(
        kernel,
        out_shape=jax.ShapeDtypeStruct((2, TR, TC), bf16),
        in_specs=[any_space] * 4 + [smem] * 2,
        out_specs=pl.BlockSpec(memory_space=pltpu.VMEM),
        scratch_shapes=[
            vmem((2, TR, TC), f32),
            vmem((2, 2, W, W), f32),
            vmem((2, W, W), bf16),
            vmem((2, W, W), bf16),
            vmem((4, 2, 2, W, W), bf16),
            vmem((2, TR + W, TC + W), bf16),
            vmem((3, 3, 8, 128), i32),
            vmem((W, 2 * W), bf16),
            vmem((2 * W, 2 * W), bf16),
            vmem((2 * W, 2 * W), bf16),
            vmem((2 * W, W), bf16),
            vmem((W, TR + W), bf16),
            vmem((TC + W, W), bf16),
            vmem((TR + W, W), bf16),
            vmem((W, TC + W), bf16),
            vmem((2, W, W), f32),
            vmem((2, 2 * W, W), bf16),
            vmem((W, 2 * W), bf16),
            vmem((4, W, 2 * W), f32),
            vmem((HW, W), f32),
            vmem((W, W), f32),
            vmem((W, 2 * W), bf16),
            vmem((2, W, W), bf16),
            vmem((2, 2 * W, W), f32),
            vmem((2, W, W), f32),
            vmem((2, TR + W, TC + W), bf16),
            vmem((2, 2, HW, TC + W), bf16),
            vmem((2, 2, TR, HW), bf16),
            vmem((2, 2, TR, HW), bf16),
            vmem((2, TR, TC + W), f32),
            vmem((4, 2, Q, TC), f32),
            vmem((4, 2, Q, TC), bf16),
            vmem((3, 2, Q, TC), bf16),
            vmem((4, 2, Q, TC), bf16),
            vmem((Q, TC), f32),
            pltpu.SemaphoreType.DMA((4,)),
            pltpu.SemaphoreType.DMA((34,)),
            pltpu.SemaphoreType.DMA((34,)),
        ],
        compiler_params=pltpu.CompilerParams(
            collective_id=0, has_side_effects=True, vmem_limit_bytes=56 * 1024 * 1024
        ),
        name="object_update",
    )(object_field, probe, amplitudes, dft_tables(), centers, live)
    return object_field + update.astype(f32)


def solution(mesh):
    return jax.shard_map(
        on_device,
        mesh=mesh,
        in_specs=(
            P(None, "tx", "ty"),
            P(None, "mode", None, None),
            P("tx", "ty", None, None, None),
            P("tx", "ty", None, None),
            P("tx", "ty"),
        ),
        out_specs=P(None, "tx", "ty"),
        check_vma=False,
    )
```

```python
import math

import jax
import jax.numpy as jnp
import numpy as np
from jax import lax
from jax.experimental import pallas as pl
from jax.experimental.pallas import tpu as pltpu
from jax.sharding import PartitionSpec as P

power_floor = 0.01
regularizer = 0.1
W = 256
HW = 128
TR = 128
TC = 256
Q = 32
f32 = jnp.float32
bf16 = jnp.bfloat16
i32 = jnp.int32
MESH = pl.DeviceIdType.MESH


def dft_tables():
    line = np.arange(W)
    angle = ((line[:, None] * line[None, :]) % W).astype(np.float32) * np.float32(2.0 * math.pi / W)
    scaling = np.float32(1.0 / math.sqrt(W))
    return jnp.asarray(
        np.stack([np.cos(angle) * scaling, -np.sin(angle) * scaling]).astype(np.float32)
    ).astype(bf16)


def dot(a, b):
    return jnp.dot(a, b, preferred_element_type=f32)


def one_hot(cond):
    return jnp.where(cond, 1.0, 0.0).astype(bf16)


def iota(shape, dim):
    return lax.broadcasted_iota(i32, shape, dim)


def kernel(
    obj_hbm,
    probe_hbm,
    amp_hbm,
    table_hbm,
    centers_ref,
    live_ref,
    out_ref,
    obj_v,
    probe_v,
    amp_v,
    tab,
    pb,
    pad,
    ib,
    mat_a,
    mat_b,
    mat_bc,
    mat_d,
    sel_p,
    sel_s,
    sel_pt,
    sel_st,
    patch,
    x_s,
    h_s,
    far_s,
    pow_s,
    wt,
    fix_s,
    r_s,
    back_s,
    grad,
    ext,
    zrecv,
    xsend,
    xrecv,
    mid,
    core_s,
    rs_s,
    rs_r,
    ag_s,
    wq,
    wt_low,
    sel_near,
    local_sem,
    send,
    recv,
):
    tx, ty, m = lax.axis_index("tx"), lax.axis_index("ty"), lax.axis_index("mode")
    nx, ny, nm = lax.axis_size("tx"), lax.axis_size("ty"), lax.axis_size("mode")
    half_ny = ny // 2
    c = lax.rem(tx, 2)
    slot = m // 2
    part = lax.rem(m, 2)

    def at(tx_at, ty_at, m_at):
        return (tx_at, ty_at, m_at)

    right_ty = lax.rem(ty + 1, ny)
    left_ty = lax.rem(ty + ny - 1, ny)
    right_m = jnp.where(lax.rem(ty, half_ny) == half_ny - 1, nm - 1 - m, m)
    left_m = jnp.where(lax.rem(ty, half_ny) == 0, nm - 1 - m, m)
    right = at(tx, right_ty, right_m)
    left = at(tx, left_ty, left_m)
    up = at(lax.rem(tx + nx - 1, nx), ty, m)
    down = at(lax.rem(tx + 1, nx), ty, m)
    partner = at(tx + 1 - 2 * c, ty, m)
    far_ty = lax.rem(ty + half_ny, ny)
    ring_up = at(tx, jnp.where(m == nm - 1, far_ty, ty), lax.rem(m + 1, nm))
    ring_down = at(tx, jnp.where(m == 0, far_ty, ty), lax.rem(m + nm - 1, nm))
    mates = [at(tx, ty, lax.rem(m + d, nm)) for d in (1, 2, 3)]

    def remote(index, src, dst, to):
        return pltpu.make_async_remote_copy(
            src_ref=src,
            dst_ref=dst,
            send_sem=send.at[index],
            recv_sem=recv.at[index],
            device_id=to,
            device_id_type=MESH,
        )

    started = []

    def go(index, src, dst, to):
        copy = remote(index, src, dst, to)
        copy.start()
        started.append(copy)
        return copy

    loads = [
        pltpu.make_async_copy(obj_hbm, obj_v, local_sem.at[0]),
        pltpu.make_async_copy(probe_hbm, probe_v, local_sem.at[1]),
        pltpu.make_async_copy(table_hbm, tab, local_sem.at[2]),
        pltpu.make_async_copy(amp_hbm.at[0, 0], amp_v, local_sem.at[3]),
    ]
    for load in loads:
        load.start()

    barrier = pltpu.get_barrier_semaphore()
    meets = [left, right, up, down, ring_up, ring_down, *mates]
    for to in meets:
        pl.semaphore_signal(barrier, inc=1, device_id=to, device_id_type=MESH)

    row = iota((8, 128), 0)
    ints = jnp.zeros((8, 128), i32)
    for at_row, value in enumerate(
        [
            centers_ref[0, 0, 0, 0],
            centers_ref[0, 0, 0, 1],
            centers_ref[0, 0, 1, 0],
            centers_ref[0, 0, 1, 1],
            live_ref[0, 0],
        ]
    ):
        ints = jnp.where(row == at_row, value, ints)
    ib[1, 1] = ints

    loads[0].wait()
    for p in range(2):
        pad[p, HW : HW + TR, HW : HW + TC] = obj_v[p].astype(bf16)
    pl.semaphore_wait(barrier, len(meets))

    mid_rows = pl.ds(HW, TR)
    top_rows = pl.ds(0, HW)
    low_rows = pl.ds(HW + TR, HW)
    mid_cols = pl.ds(HW, TC)
    left_cols = pl.ds(0, HW)
    right_cols = pl.ds(HW + TC, HW)
    to_left = go(0, pad.at[:, mid_rows, pl.ds(HW, HW)], pad.at[:, mid_rows, right_cols], left)
    to_right = go(1, pad.at[:, mid_rows, pl.ds(TC, HW)], pad.at[:, mid_rows, left_cols], right)
    ints_left = go(2, ib.at[1, 1], ib.at[1, 2], left)
    ints_right = go(3, ib.at[1, 1], ib.at[1, 0], right)
    z_up = go(4, pad.at[:, mid_rows, mid_cols], pad.at[:, low_rows, mid_cols], up)
    z_down = go(5, pad.at[:, mid_rows, mid_cols], pad.at[:, top_rows, mid_cols], down)

    loads[1].wait()
    for p in range(2):
        pb[0, 0, p] = probe_v[p, c].astype(bf16)
    ring = {}
    ring[3, 0] = go(12, pb.at[0, 0, 0], pb.at[3, 0, 0], ring_up)
    ring[1, 1] = go(13, pb.at[0, 0, 1], pb.at[1, 0, 1], ring_down)
    ring[3, 1] = go(14, pb.at[0, 0, 1], pb.at[3, 0, 1], ring_up)
    ring[1, 0] = go(15, pb.at[0, 0, 0], pb.at[1, 0, 0], ring_down)
    for p in range(2):
        pb[0, 1, p] = probe_v[p, 1 - c].astype(bf16)

    loads[2].wait()
    fr, fi = tab[0], tab[1]
    rows_here = pl.ds(pl.multiple_of(part * HW, HW), HW)
    fr_half, fi_half = tab[0, rows_here, :], tab[1, rows_here, :]
    mat_a[0:HW, 0:W] = fr_half
    mat_a[0:HW, W : 2 * W] = -fi_half
    mat_a[HW:W, 0:W] = fi_half
    mat_a[HW:W, W : 2 * W] = fr_half
    mat_b[0:W, 0:W] = fr
    mat_b[0:W, W : 2 * W] = fi
    mat_b[W : 2 * W, 0:W] = -fi
    mat_b[W : 2 * W, W : 2 * W] = fr
    mat_bc[0:W, 0:W] = fr
    mat_bc[0:W, W : 2 * W] = -fi
    mat_bc[W : 2 * W, 0:W] = fi
    mat_bc[W : 2 * W, W : 2 * W] = fr
    cols_here = pl.ds(pl.multiple_of(part * HW, HW), HW)
    fr_cols, fi_cols = tab[0, :, cols_here], tab[1, :, cols_here]
    mat_d[0:W, 0:HW] = fr_cols
    mat_d[0:W, HW:W] = fi_cols
    mat_d[W : 2 * W, 0:HW] = -fi_cols
    mat_d[W : 2 * W, HW:W] = fr_cols

    row_at = jnp.where(slot == 0, centers_ref[0, 0, 0, 0], centers_ref[0, 0, 1, 0])
    col_at = jnp.where(slot == 0, centers_ref[0, 0, 0, 1], centers_ref[0, 0, 1, 1])
    row_from = jnp.where(tx == 0, HW, 0)
    row_to = jnp.where(tx == nx - 1, HW + TR, TR + W)
    col_from = jnp.where(ty == 0, HW, 0)
    col_to = jnp.where(ty == ny - 1, HW + TC, TC + W)

    def selection(shape, outer, base, start, stop):
        big, small = iota(shape, outer), iota(shape, 1 - outer)
        return one_hot((big == small + base) & (big >= start) & (big < stop))

    sel_p[...] = selection((W, TR + W), 1, row_at, row_from, row_to)
    sel_pt[...] = selection((TR + W, W), 0, row_at, row_from, row_to)
    sel_s[...] = selection((TC + W, W), 0, col_at, col_from, col_to)
    sel_st[...] = selection((W, TC + W), 1, col_at, col_from, col_to)

    side = {}

    def pass_on(index, d, p):
        side[d, p] = go(index, pb.at[d, 0, p], pb.at[d, 1, p], partner)

    to_left.wait_recv()
    to_right.wait_recv()
    z_sides = [
        go(6, pad.at[:, mid_rows, left_cols], pad.at[:, low_rows, left_cols], up),
        go(7, pad.at[:, mid_rows, right_cols], pad.at[:, low_rows, right_cols], up),
        go(8, pad.at[:, mid_rows, left_cols], pad.at[:, top_rows, left_cols], down),
        go(9, pad.at[:, mid_rows, right_cols], pad.at[:, top_rows, right_cols], down),
    ]
    ring[3, 0].wait_recv()
    ring[2, 0] = go(16, pb.at[3, 0, 0], pb.at[2, 0, 0], ring_up)
    ring[1, 1].wait_recv()
    ring[2, 1] = go(17, pb.at[1, 0, 1], pb.at[2, 0, 1], ring_down)
    pass_on(18, 3, 0)
    pass_on(19, 1, 1)

    ints_left.wait_recv()
    ints_right.wait_recv()
    ints_up = go(10, ib.at[1], ib.at[2], up)
    ints_down = go(11, ib.at[1], ib.at[0], down)

    ring[3, 1].wait_recv()
    pass_on(20, 3, 1)
    ring[1, 0].wait_recv()
    pass_on(21, 1, 0)

    z_up.wait_recv()
    z_down.wait_recv()
    for copy in z_sides:
        copy.wait_recv()
    for p in range(2):
        shifted = dot(sel_p[...], pad[p]).astype(bf16)
        patch[p] = dot(shifted, sel_s[...])

    ring[2, 0].wait_recv()
    pass_on(22, 2, 0)
    ring[2, 1].wait_recv()
    pass_on(23, 2, 1)

    chunk = 32

    def forward(d, first):
        def exits(i, carry):
            at_rows = pl.ds(pl.multiple_of(i * chunk, chunk), chunk)
            low_rows_at = pl.ds(pl.multiple_of(W + i * chunk, chunk), chunk)
            o_r, o_i = patch[0, at_rows, :], patch[1, at_rows, :]
            weight = jnp.zeros((chunk, W), f32) if first else wt[at_rows, :]
            for j in range(2):
                p_r = pb[d, j, 0, at_rows, :].astype(f32)
                p_i = pb[d, j, 1, at_rows, :].astype(f32)
                x_s[j, at_rows, :] = (p_r * o_r - p_i * o_i).astype(bf16)
                x_s[j, low_rows_at, :] = (p_r * o_i + p_i * o_r).astype(bf16)
                weight = weight + (p_r * p_r + p_i * p_i)
            wt[at_rows, :] = weight
            return carry

        lax.fori_loop(0, W // chunk, exits, 0)
        for j in range(2):
            half = dot(mat_a[...], x_s[j]).astype(bf16)
            h_s[j * HW : (j + 1) * HW, 0:W] = half[0:HW]
            h_s[j * HW : (j + 1) * HW, W : 2 * W] = half[HW:W]
        far_s[d] = dot(h_s[...], mat_b[...])

        def powers(i, carry):
            at_rows = pl.ds(pl.multiple_of(i * chunk, chunk), chunk)
            next_rows = pl.ds(pl.multiple_of(HW + i * chunk, chunk), chunk)
            total = jnp.zeros((chunk, W), f32) if first else pow_s[at_rows, :]
            for rows in (at_rows, next_rows):
                a, b = far_s[d, rows, 0:W], far_s[d, rows, W : 2 * W]
                total = total + (a * a + b * b)
            pow_s[at_rows, :] = total
            return carry

        lax.fori_loop(0, HW // chunk, powers, 0)

    forward(0, True)
    side[3, 0].wait_recv()
    side[3, 1].wait_recv()
    forward(3, False)
    side[1, 1].wait_recv()
    side[1, 0].wait_recv()
    forward(1, False)
    side[2, 0].wait_recv()
    side[2, 1].wait_recv()
    forward(2, False)

    loads[3].wait()
    amplitude = amp_v[slot, rows_here, :].astype(f32)
    pow_s[...] = amplitude / jnp.sqrt(pow_s[...] + power_floor)

    def backward(d, carry):
        def fixes(i, carry):
            at_rows = pl.ds(pl.multiple_of(i * chunk, chunk), chunk)
            next_rows = pl.ds(pl.multiple_of(HW + i * chunk, chunk), chunk)
            factor = pow_s[at_rows, :]
            for rows in (at_rows, next_rows):
                fix_s[rows, 0:W] = (far_s[d, rows, 0:W] * factor).astype(bf16)
                fix_s[rows, W : 2 * W] = (far_s[d, rows, W : 2 * W] * factor).astype(bf16)
            return carry

        lax.fori_loop(0, HW // chunk, fixes, 0)
        half = dot(fix_s[...], mat_bc[...]).astype(bf16)
        for j in range(2):
            r_s[j, 0:HW, :] = half[j * HW : (j + 1) * HW, 0:W]
            r_s[j, HW:W, :] = half[j * HW : (j + 1) * HW, W : 2 * W]
        for j in range(2):
            back_s[j] = dot(mat_d[...], r_s[j])

        def grads(i, carry):
            at_rows = pl.ds(pl.multiple_of(i * chunk, chunk), chunk)
            low_rows_at = pl.ds(pl.multiple_of(W + i * chunk, chunk), chunk)
            g_r, g_i = grad[0, at_rows, :], grad[1, at_rows, :]
            for j in range(2):
                p_r = pb[d, j, 0, at_rows, :].astype(f32)
                p_i = pb[d, j, 1, at_rows, :].astype(f32)
                b_r, b_i = back_s[j, at_rows, :], back_s[j, low_rows_at, :]
                g_r = g_r + (p_r * b_r + p_i * b_i)
                g_i = g_i + (p_r * b_i - p_i * b_r)
            grad[0, at_rows, :] = g_r
            grad[1, at_rows, :] = g_i
            return carry

        lax.fori_loop(0, W // chunk, grads, 0)
        return carry

    for p in range(2):
        grad[p] = -0.5 * wt[...] * patch[p]
    lax.fori_loop(0, 4, backward, 0)

    counts = slot < live_ref[0, 0]
    folds = []
    for p in range(2):
        low = jnp.where(counts, grad[p], 0.0).astype(bf16)
        ext[p] = dot(sel_pt[...], low).astype(bf16)
        folds.append(
            (
                go(24 + 2 * p, ext.at[p, top_rows, :], zrecv.at[0, p], up),
                go(25 + 2 * p, ext.at[p, low_rows, :], zrecv.at[1, p], down),
            )
        )

    def weight_rows(a):
        total = jnp.zeros((Q, TC), f32) if a == 0 else wq[...]
        for b in range(3):
            inside = (
                jnp.where(tx + (a - 1) >= 0, 1, 0)
                * jnp.where(tx + (a - 1) < nx, 1, 0)
                * jnp.where(ty + (b - 1) >= 0, 1, 0)
                * jnp.where(ty + (b - 1) < ny, 1, 0)
            )
            block = ib[a, b]
            alive = block[4:5, 0:1] * inside
            for s in range(2):
                row_of = m * Q + HW - HW * (a - 1) - block[2 * s : 2 * s + 1, 0:1]
                col_of = HW - TC * (b - 1) - block[2 * s + 1 : 2 * s + 2, 0:1]
                pick = one_hot((iota((Q, W), 1) == iota((Q, W), 0) + row_of) & (alive > s))
                place = one_hot(iota((W, TC), 0) == iota((W, TC), 1) + col_of)
                picked = dot(pick, wt_low[...]).astype(bf16)
                total = total + dot(picked, place)
        wq[...] = total

    wt_low[...] = wt[...].astype(bf16)
    ints_up.wait_recv()
    ints_down.wait_recv()
    for index, a in ((0, 2), (1, 0)):
        block = ib[a, 1]
        col_there = jnp.where(slot == 0, block[1:2, 0:1], block[3:4, 0:1])
        sel_near[index] = selection((W, TC + W), 1, col_there, col_from, col_to)
    for p in range(2):
        mid[p] = dot(ext[p, HW : HW + TR, :], sel_st[...])

    columns = []
    for p in range(2):
        for copy in folds[p]:
            copy.wait_recv()
        mid[p] = mid[p] + (
            dot(zrecv[0, p], sel_near[0]) + dot(zrecv[1, p], sel_near[1])
        )
        xsend[p, 0] = mid[p, :, 0:HW].astype(bf16)
        xsend[p, 1] = mid[p, :, HW + TC :].astype(bf16)
        columns.append(
            (
                go(28 + 2 * p, xsend.at[p, 0], xrecv.at[p, 1], left),
                go(29 + 2 * p, xsend.at[p, 1], xrecv.at[p, 0], right),
            )
        )
    weight_rows(0)
    weight_rows(1)

    sums = []
    for p in range(2):
        for copy in columns[p]:
            copy.wait_recv()
        for q in range(4):
            rows = slice(q * Q, (q + 1) * Q)
            core_s[p, q, :, 0:HW] = mid[p, rows, HW : 2 * HW] + xrecv[p, 0, rows, :].astype(f32)
            core_s[p, q, :, HW:TC] = mid[p, rows, 2 * HW : 3 * HW] + xrecv[p, 1, rows, :].astype(f32)
            rs_s[p, q] = core_s[p, q].astype(bf16)
        sums.append(
            [
                go(31 + 3 * p + d, rs_s.at[p, lax.rem(m + d, nm)], rs_r.at[p, d - 1], mates[d - 1])
                for d in (1, 2, 3)
            ]
        )
    weight_rows(2)
    scale = wq[...] + regularizer

    gathers = []
    for p in range(2):
        total = core_s[p, m]
        for d in (1, 2, 3):
            sums[p][d - 1].wait_recv()
            total = total + rs_r[p, d - 1].astype(f32)
        ag_s[p, m] = (total / scale).astype(bf16)
        gathers.append(
            [go(37 + 3 * p + d, ag_s.at[p, m], ag_s.at[p, m], mates[d - 1]) for d in (1, 2, 3)]
        )
    for p in range(2):
        for copy in gathers[p]:
            copy.wait_recv()
        for q in range(4):
            out_ref[p, q * Q : (q + 1) * Q, :] = ag_s[p, q]
    for copy in started:
        copy.wait_send()


def on_device(object_field, probe, amplitudes, centers, live):
    any_space = pl.BlockSpec(memory_space=pl.ANY)
    smem = pl.BlockSpec(memory_space=pltpu.SMEM)
    vmem = pltpu.VMEM
    update = pl.pallas_call(
        kernel,
        out_shape=jax.ShapeDtypeStruct((2, TR, TC), bf16),
        in_specs=[any_space] * 4 + [smem] * 2,
        out_specs=pl.BlockSpec(memory_space=pltpu.VMEM),
        scratch_shapes=[
            vmem((2, TR, TC), f32),
            vmem((2, 2, W, W), f32),
            vmem((2, W, W), bf16),
            vmem((2, W, W), bf16),
            vmem((4, 2, 2, W, W), bf16),
            vmem((2, TR + W, TC + W), bf16),
            vmem((3, 3, 8, 128), i32),
            vmem((W, 2 * W), bf16),
            vmem((2 * W, 2 * W), bf16),
            vmem((2 * W, 2 * W), bf16),
            vmem((2 * W, W), bf16),
            vmem((W, TR + W), bf16),
            vmem((TC + W, W), bf16),
            vmem((TR + W, W), bf16),
            vmem((W, TC + W), bf16),
            vmem((2, W, W), f32),
            vmem((2, 2 * W, W), bf16),
            vmem((W, 2 * W), bf16),
            vmem((4, W, 2 * W), f32),
            vmem((HW, W), f32),
            vmem((W, W), f32),
            vmem((W, 2 * W), bf16),
            vmem((2, W, W), bf16),
            vmem((2, 2 * W, W), f32),
            vmem((2, W, W), f32),
            vmem((2, TR + W, W), bf16),
            vmem((2, 2, HW, W), bf16),
            vmem((2, 2, TR, HW), bf16),
            vmem((2, 2, TR, HW), bf16),
            vmem((2, TR, TC + W), f32),
            vmem((2, 4, Q, TC), f32),
            vmem((2, 4, Q, TC), bf16),
            vmem((2, 3, Q, TC), bf16),
            vmem((2, 4, Q, TC), bf16),
            vmem((Q, TC), f32),
            vmem((W, W), bf16),
            vmem((2, W, TC + W), bf16),
            pltpu.SemaphoreType.DMA((4,)),
            pltpu.SemaphoreType.DMA((44,)),
            pltpu.SemaphoreType.DMA((44,)),
        ],
        compiler_params=pltpu.CompilerParams(
            collective_id=0, has_side_effects=True, vmem_limit_bytes=56 * 1024 * 1024
        ),
        name="object_update",
    )(object_field, probe, amplitudes, dft_tables(), centers, live)
    return object_field + update.astype(f32)


def solution(mesh):
    return jax.shard_map(
        on_device,
        mesh=mesh,
        in_specs=(
            P(None, "tx", "ty"),
            P(None, "mode", None, None),
            P("tx", "ty", None, None, None),
            P("tx", "ty", None, None),
            P("tx", "ty"),
        ),
        out_specs=P(None, "tx", "ty"),
        check_vma=False,
    )
```

```python
import math

import jax
import jax.numpy as jnp
import numpy as np
from jax import lax
from jax.experimental import pallas as pl
from jax.experimental.pallas import tpu as pltpu
from jax.sharding import PartitionSpec as P

power_floor = 0.01
regularizer = 0.1
W = 256
HW = 128
TR = 128
TC = 256
Q = 32
f32 = jnp.float32
bf16 = jnp.bfloat16
i32 = jnp.int32
MESH = pl.DeviceIdType.MESH


def dft_tables():
    line = np.arange(W)
    angle = ((line[:, None] * line[None, :]) % W).astype(np.float32) * np.float32(2.0 * math.pi / W)
    scaling = np.float32(1.0 / math.sqrt(W))
    return jnp.asarray(
        np.stack([np.cos(angle) * scaling, -np.sin(angle) * scaling]).astype(np.float32)
    ).astype(bf16)


def dot(a, b):
    return jnp.dot(a, b, preferred_element_type=f32)


def one_hot(cond):
    return jnp.where(cond, 1.0, 0.0).astype(bf16)


def iota(shape, dim):
    return lax.broadcasted_iota(i32, shape, dim)


def kernel(
    obj_hbm,
    probe_hbm,
    amp_hbm,
    table_hbm,
    centers_hbm,
    live_hbm,
    out_ref,
    obj_v,
    probe_v,
    amp_v,
    tab,
    pb,
    pad,
    ib,
    mat_a,
    mat_b,
    mat_bc,
    mat_d,
    sel_p,
    sel_s,
    sel_pt,
    sel_st,
    patch,
    x_s,
    h_s,
    far_s,
    pow_s,
    wt,
    fix_s,
    r_s,
    back_s,
    grad,
    ext,
    zrecv,
    xsend,
    xrecv,
    mid,
    core_s,
    rs_s,
    rs_r,
    ag_s,
    wq,
    wt_low,
    sel_near,
    centers_ref,
    live_ref,
    local_sem,
    send,
    recv,
):
    tx, ty, m = lax.axis_index("tx"), lax.axis_index("ty"), lax.axis_index("mode")
    nx, ny, nm = lax.axis_size("tx"), lax.axis_size("ty"), lax.axis_size("mode")
    half_ny = ny // 2
    c = lax.rem(tx, 2)
    slot = m // 2
    part = lax.rem(m, 2)

    def at(tx_at, ty_at, m_at):
        return (tx_at, ty_at, m_at)

    right_ty = lax.rem(ty + 1, ny)
    left_ty = lax.rem(ty + ny - 1, ny)
    right_m = jnp.where(lax.rem(ty, half_ny) == half_ny - 1, nm - 1 - m, m)
    left_m = jnp.where(lax.rem(ty, half_ny) == 0, nm - 1 - m, m)
    right = at(tx, right_ty, right_m)
    left = at(tx, left_ty, left_m)
    up = at(lax.rem(tx + nx - 1, nx), ty, m)
    down = at(lax.rem(tx + 1, nx), ty, m)
    partner = at(tx + 1 - 2 * c, ty, m)
    far_ty = lax.rem(ty + half_ny, ny)
    ring_up = at(tx, jnp.where(m == nm - 1, far_ty, ty), lax.rem(m + 1, nm))
    ring_down = at(tx, jnp.where(m == 0, far_ty, ty), lax.rem(m + nm - 1, nm))
    mates = [at(tx, ty, lax.rem(m + d, nm)) for d in (1, 2, 3)]

    def remote(index, src, dst, to):
        return pltpu.make_async_remote_copy(
            src_ref=src,
            dst_ref=dst,
            send_sem=send.at[index],
            recv_sem=recv.at[index],
            device_id=to,
            device_id_type=MESH,
        )

    started = []

    def go(index, src, dst, to):
        copy = remote(index, src, dst, to)
        copy.start()
        started.append(copy)
        return copy

    loads = [
        pltpu.make_async_copy(obj_hbm, obj_v, local_sem.at[0]),
        pltpu.make_async_copy(probe_hbm, probe_v, local_sem.at[1]),
        pltpu.make_async_copy(table_hbm, tab, local_sem.at[2]),
        pltpu.make_async_copy(amp_hbm.at[0, 0], amp_v, local_sem.at[3]),
        pltpu.make_async_copy(centers_hbm, centers_ref, local_sem.at[4]),
        pltpu.make_async_copy(live_hbm, live_ref, local_sem.at[5]),
    ]
    for load in loads:
        load.start()

    barrier = pltpu.get_barrier_semaphore()
    meets = [left, right, up, down, ring_up, ring_down, *mates]
    for to in meets:
        pl.semaphore_signal(barrier, inc=1, device_id=to, device_id_type=MESH)

    loads[0].wait()
    for p in range(2):
        pad[p, HW : HW + TR, HW : HW + TC] = obj_v[p].astype(bf16)
    pl.semaphore_wait(barrier, len(meets))

    mid_rows = pl.ds(HW, TR)
    top_rows = pl.ds(0, HW)
    low_rows = pl.ds(HW + TR, HW)
    mid_cols = pl.ds(HW, TC)
    left_cols = pl.ds(0, HW)
    right_cols = pl.ds(HW + TC, HW)
    to_left, to_right = [], []
    for p in range(2):
        to_left.append(
            go(p, pad.at[p, mid_rows, pl.ds(HW, HW)], pad.at[p, mid_rows, right_cols], left)
        )
        to_right.append(
            go(44 + p, pad.at[p, mid_rows, pl.ds(TC, HW)], pad.at[p, mid_rows, left_cols], right)
        )
    z_up = go(4, pad.at[:, mid_rows, mid_cols], pad.at[:, low_rows, mid_cols], up)
    z_down = go(5, pad.at[:, mid_rows, mid_cols], pad.at[:, top_rows, mid_cols], down)

    loads[4].wait()
    loads[5].wait()
    row = iota((8, 128), 0)
    ints = jnp.zeros((8, 128), i32)
    for at_row, value in enumerate(
        [
            centers_ref[0, 0, 0, 0],
            centers_ref[0, 0, 0, 1],
            centers_ref[0, 0, 1, 0],
            centers_ref[0, 0, 1, 1],
            live_ref[0, 0],
        ]
    ):
        ints = jnp.where(row == at_row, value, ints)
    ib[1, 1] = ints

    ints_left = go(2, ib.at[1, 1], ib.at[1, 2], left)
    ints_right = go(3, ib.at[1, 1], ib.at[1, 0], right)

    loads[1].wait()
    for p in range(2):
        pb[0, 0, p] = probe_v[p, c].astype(bf16)
    ring = {}
    ring[3, 0] = go(12, pb.at[0, 0, 0], pb.at[3, 0, 0], ring_up)
    ring[1, 1] = go(13, pb.at[0, 0, 1], pb.at[1, 0, 1], ring_down)
    ring[3, 1] = go(14, pb.at[0, 0, 1], pb.at[3, 0, 1], ring_up)
    ring[1, 0] = go(15, pb.at[0, 0, 0], pb.at[1, 0, 0], ring_down)
    for p in range(2):
        pb[0, 1, p] = probe_v[p, 1 - c].astype(bf16)

    loads[2].wait()
    fr, fi = tab[0], tab[1]
    rows_here = pl.ds(pl.multiple_of(part * HW, HW), HW)
    fr_half, fi_half = tab[0, rows_here, :], tab[1, rows_here, :]
    mat_a[0:HW, 0:W] = fr_half
    mat_a[0:HW, W : 2 * W] = -fi_half
    mat_a[HW:W, 0:W] = fi_half
    mat_a[HW:W, W : 2 * W] = fr_half
    mat_b[0:W, 0:W] = fr
    mat_b[0:W, W : 2 * W] = fi
    mat_b[W : 2 * W, 0:W] = -fi
    mat_b[W : 2 * W, W : 2 * W] = fr
    mat_bc[0:W, 0:W] = fr
    mat_bc[0:W, W : 2 * W] = -fi
    mat_bc[W : 2 * W, 0:W] = fi
    mat_bc[W : 2 * W, W : 2 * W] = fr
    cols_here = pl.ds(pl.multiple_of(part * HW, HW), HW)
    fr_cols, fi_cols = tab[0, :, cols_here], tab[1, :, cols_here]
    mat_d[0:W, 0:HW] = fr_cols
    mat_d[0:W, HW:W] = fi_cols
    mat_d[W : 2 * W, 0:HW] = -fi_cols
    mat_d[W : 2 * W, HW:W] = fr_cols

    row_at = jnp.where(slot == 0, centers_ref[0, 0, 0, 0], centers_ref[0, 0, 1, 0])
    col_at = jnp.where(slot == 0, centers_ref[0, 0, 0, 1], centers_ref[0, 0, 1, 1])
    row_from = jnp.where(tx == 0, HW, 0)
    row_to = jnp.where(tx == nx - 1, HW + TR, TR + W)
    col_from = jnp.where(ty == 0, HW, 0)
    col_to = jnp.where(ty == ny - 1, HW + TC, TC + W)

    def selection(shape, outer, base, start, stop):
        big, small = iota(shape, outer), iota(shape, 1 - outer)
        return one_hot((big == small + base) & (big >= start) & (big < stop))

    sel_p[...] = selection((W, TR + W), 1, row_at, row_from, row_to)
    sel_pt[...] = selection((TR + W, W), 0, row_at, row_from, row_to)
    sel_s[...] = selection((TC + W, W), 0, col_at, col_from, col_to)
    sel_st[...] = selection((W, TC + W), 1, col_at, col_from, col_to)

    side = {}

    def pass_on(index, d, p):
        side[d, p] = go(index, pb.at[d, 0, p], pb.at[d, 1, p], partner)

    z_sides = []
    for p in range(2):
        to_left[p].wait_recv()
        to_right[p].wait_recv()
        for i, cols in enumerate((left_cols, right_cols)):
            here = pad.at[p, mid_rows, cols]
            z_sides.append(go(6 + 2 * p + i, here, pad.at[p, low_rows, cols], up))
            z_sides.append(go(46 + 2 * p + i, here, pad.at[p, top_rows, cols], down))
    ring[3, 0].wait_recv()
    ring[2, 0] = go(16, pb.at[3, 0, 0], pb.at[2, 0, 0], ring_up)
    ring[1, 1].wait_recv()
    ring[2, 1] = go(17, pb.at[1, 0, 1], pb.at[2, 0, 1], ring_down)
    pass_on(18, 3, 0)
    pass_on(19, 1, 1)

    ints_left.wait_recv()
    ints_right.wait_recv()
    ints_up = go(10, ib.at[1], ib.at[2], up)
    ints_down = go(11, ib.at[1], ib.at[0], down)

    ring[3, 1].wait_recv()
    pass_on(20, 3, 1)
    ring[1, 0].wait_recv()
    pass_on(21, 1, 0)

    z_up.wait_recv()
    z_down.wait_recv()
    for copy in z_sides:
        copy.wait_recv()
    for p in range(2):
        shifted = dot(sel_p[...], pad[p]).astype(bf16)
        patch[p] = dot(shifted, sel_s[...])

    ring[2, 0].wait_recv()
    pass_on(22, 2, 0)
    ring[2, 1].wait_recv()
    pass_on(23, 2, 1)

    chunk = 32

    def forward(d, first):
        def exits(i, carry):
            at_rows = pl.ds(pl.multiple_of(i * chunk, chunk), chunk)
            low_rows_at = pl.ds(pl.multiple_of(W + i * chunk, chunk), chunk)
            o_r, o_i = patch[0, at_rows, :], patch[1, at_rows, :]
            weight = jnp.zeros((chunk, W), f32) if first else wt[at_rows, :]
            for j in range(2):
                p_r = pb[d, j, 0, at_rows, :].astype(f32)
                p_i = pb[d, j, 1, at_rows, :].astype(f32)
                x_s[j, at_rows, :] = (p_r * o_r - p_i * o_i).astype(bf16)
                x_s[j, low_rows_at, :] = (p_r * o_i + p_i * o_r).astype(bf16)
                weight = weight + (p_r * p_r + p_i * p_i)
            wt[at_rows, :] = weight
            return carry

        lax.fori_loop(0, W // chunk, exits, 0)
        for j in range(2):
            half = dot(mat_a[...], x_s[j]).astype(bf16)
            h_s[j * HW : (j + 1) * HW, 0:W] = half[0:HW]
            h_s[j * HW : (j + 1) * HW, W : 2 * W] = half[HW:W]
        far_s[d] = dot(h_s[...], mat_b[...])

        def powers(i, carry):
            at_rows = pl.ds(pl.multiple_of(i * chunk, chunk), chunk)
            next_rows = pl.ds(pl.multiple_of(HW + i * chunk, chunk), chunk)
            total = jnp.zeros((chunk, W), f32) if first else pow_s[at_rows, :]
            for rows in (at_rows, next_rows):
                a, b = far_s[d, rows, 0:W], far_s[d, rows, W : 2 * W]
                total = total + (a * a + b * b)
            pow_s[at_rows, :] = total
            return carry

        lax.fori_loop(0, HW // chunk, powers, 0)

    forward(0, True)
    side[3, 0].wait_recv()
    side[3, 1].wait_recv()
    forward(3, False)
    side[1, 1].wait_recv()
    side[1, 0].wait_recv()
    forward(1, False)
    side[2, 0].wait_recv()
    side[2, 1].wait_recv()
    forward(2, False)

    loads[3].wait()
    amplitude = amp_v[slot, rows_here, :].astype(f32)
    pow_s[...] = amplitude / jnp.sqrt(pow_s[...] + power_floor)

    def backward(d, carry):
        def fixes(i, carry):
            at_rows = pl.ds(pl.multiple_of(i * chunk, chunk), chunk)
            next_rows = pl.ds(pl.multiple_of(HW + i * chunk, chunk), chunk)
            factor = pow_s[at_rows, :]
            for rows in (at_rows, next_rows):
                fix_s[rows, 0:W] = (far_s[d, rows, 0:W] * factor).astype(bf16)
                fix_s[rows, W : 2 * W] = (far_s[d, rows, W : 2 * W] * factor).astype(bf16)
            return carry

        lax.fori_loop(0, HW // chunk, fixes, 0)
        half = dot(fix_s[...], mat_bc[...]).astype(bf16)
        for j in range(2):
            r_s[j, 0:HW, :] = half[j * HW : (j + 1) * HW, 0:W]
            r_s[j, HW:W, :] = half[j * HW : (j + 1) * HW, W : 2 * W]
        for j in range(2):
            back_s[j] = dot(mat_d[...], r_s[j])

        def grads(i, carry):
            at_rows = pl.ds(pl.multiple_of(i * chunk, chunk), chunk)
            low_rows_at = pl.ds(pl.multiple_of(W + i * chunk, chunk), chunk)
            g_r, g_i = grad[0, at_rows, :], grad[1, at_rows, :]
            for j in range(2):
                p_r = pb[d, j, 0, at_rows, :].astype(f32)
                p_i = pb[d, j, 1, at_rows, :].astype(f32)
                b_r, b_i = back_s[j, at_rows, :], back_s[j, low_rows_at, :]
                g_r = g_r + (p_r * b_r + p_i * b_i)
                g_i = g_i + (p_r * b_i - p_i * b_r)
            grad[0, at_rows, :] = g_r
            grad[1, at_rows, :] = g_i
            return carry

        lax.fori_loop(0, W // chunk, grads, 0)
        return carry

    for p in range(2):
        grad[p] = -0.5 * wt[...] * patch[p]
    lax.fori_loop(0, 4, backward, 0)

    counts = slot < live_ref[0, 0]
    folds = []
    for p in range(2):
        low = jnp.where(counts, grad[p], 0.0).astype(bf16)
        ext[p] = dot(sel_pt[...], low).astype(bf16)
        folds.append(
            (
                go(24 + 2 * p, ext.at[p, top_rows, :], zrecv.at[0, p], up),
                go(25 + 2 * p, ext.at[p, low_rows, :], zrecv.at[1, p], down),
            )
        )

    def weight_rows(a):
        total = jnp.zeros((Q, TC), f32) if a == 0 else wq[...]
        for b in range(3):
            inside = (
                jnp.where(tx + (a - 1) >= 0, 1, 0)
                * jnp.where(tx + (a - 1) < nx, 1, 0)
                * jnp.where(ty + (b - 1) >= 0, 1, 0)
                * jnp.where(ty + (b - 1) < ny, 1, 0)
            )
            block = ib[a, b]
            alive = block[4:5, 0:1] * inside
            for s in range(2):
                row_of = m * Q + HW - HW * (a - 1) - block[2 * s : 2 * s + 1, 0:1]
                col_of = HW - TC * (b - 1) - block[2 * s + 1 : 2 * s + 2, 0:1]
                pick = one_hot((iota((Q, W), 1) == iota((Q, W), 0) + row_of) & (alive > s))
                place = one_hot(iota((W, TC), 0) == iota((W, TC), 1) + col_of)
                picked = dot(pick, wt_low[...]).astype(bf16)
                total = total + dot(picked, place)
        wq[...] = total

    wt_low[...] = wt[...].astype(bf16)
    ints_up.wait_recv()
    ints_down.wait_recv()
    for index, a in ((0, 2), (1, 0)):
        block = ib[a, 1]
        col_there = jnp.where(slot == 0, block[1:2, 0:1], block[3:4, 0:1])
        sel_near[index] = selection((W, TC + W), 1, col_there, col_from, col_to)
    for p in range(2):
        mid[p] = dot(ext[p, HW : HW + TR, :], sel_st[...])

    columns = []
    for p in range(2):
        for copy in folds[p]:
            copy.wait_recv()
        mid[p] = mid[p] + (
            dot(zrecv[0, p], sel_near[0]) + dot(zrecv[1, p], sel_near[1])
        )
        xsend[p, 0] = mid[p, :, 0:HW].astype(bf16)
        xsend[p, 1] = mid[p, :, HW + TC :].astype(bf16)
        columns.append(
            (
                go(28 + 2 * p, xsend.at[p, 0], xrecv.at[p, 1], left),
                go(29 + 2 * p, xsend.at[p, 1], xrecv.at[p, 0], right),
            )
        )
    weight_rows(0)
    weight_rows(1)

    sums = []
    for p in range(2):
        for copy in columns[p]:
            copy.wait_recv()
        for q in range(4):
            rows = slice(q * Q, (q + 1) * Q)
            core_s[p, q, :, 0:HW] = mid[p, rows, HW : 2 * HW] + xrecv[p, 0, rows, :].astype(f32)
            core_s[p, q, :, HW:TC] = mid[p, rows, 2 * HW : 3 * HW] + xrecv[p, 1, rows, :].astype(f32)
            rs_s[p, q] = core_s[p, q].astype(bf16)
        sums.append(
            [
                go(31 + 3 * p + d, rs_s.at[p, lax.rem(m + d, nm)], rs_r.at[p, d - 1], mates[d - 1])
                for d in (1, 2, 3)
            ]
        )
    weight_rows(2)
    scale = wq[...] + regularizer

    gathers = []
    for p in range(2):
        total = core_s[p, m]
        for d in (1, 2, 3):
            sums[p][d - 1].wait_recv()
            total = total + rs_r[p, d - 1].astype(f32)
        ag_s[p, m] = (total / scale).astype(bf16)
        gathers.append(
            [go(37 + 3 * p + d, ag_s.at[p, m], ag_s.at[p, m], mates[d - 1]) for d in (1, 2, 3)]
        )
    for p in range(2):
        for copy in gathers[p]:
            copy.wait_recv()
        for q in range(4):
            out_ref[p, q * Q : (q + 1) * Q, :] = ag_s[p, q]
    for copy in started:
        copy.wait_send()


def on_device(object_field, probe, amplitudes, centers, live):
    any_space = pl.BlockSpec(memory_space=pl.ANY)
    vmem = pltpu.VMEM
    update = pl.pallas_call(
        kernel,
        out_shape=pltpu.VMEM((2, TR, TC), bf16),
        in_specs=[any_space] * 6,
        out_specs=pl.BlockSpec(memory_space=pltpu.VMEM),
        scratch_shapes=[
            vmem((2, TR, TC), f32),
            vmem((2, 2, W, W), f32),
            vmem((2, W, W), bf16),
            vmem((2, W, W), bf16),
            vmem((4, 2, 2, W, W), bf16),
            vmem((2, TR + W, TC + W), bf16),
            vmem((3, 3, 8, 128), i32),
            vmem((W, 2 * W), bf16),
            vmem((2 * W, 2 * W), bf16),
            vmem((2 * W, 2 * W), bf16),
            vmem((2 * W, W), bf16),
            vmem((W, TR + W), bf16),
            vmem((TC + W, W), bf16),
            vmem((TR + W, W), bf16),
            vmem((W, TC + W), bf16),
            vmem((2, W, W), f32),
            vmem((2, 2 * W, W), bf16),
            vmem((W, 2 * W), bf16),
            vmem((4, W, 2 * W), f32),
            vmem((HW, W), f32),
            vmem((W, W), f32),
            vmem((W, 2 * W), bf16),
            vmem((2, W, W), bf16),
            vmem((2, 2 * W, W), f32),
            vmem((2, W, W), f32),
            vmem((2, TR + W, W), bf16),
            vmem((2, 2, HW, W), bf16),
            vmem((2, 2, TR, HW), bf16),
            vmem((2, 2, TR, HW), bf16),
            vmem((2, TR, TC + W), f32),
            vmem((2, 4, Q, TC), f32),
            vmem((2, 4, Q, TC), bf16),
            vmem((2, 3, Q, TC), bf16),
            vmem((2, 4, Q, TC), bf16),
            vmem((Q, TC), f32),
            vmem((W, W), bf16),
            vmem((2, W, TC + W), bf16),
            pltpu.SMEM((1, 1, 2, 2), i32),
            pltpu.SMEM((1, 1), i32),
            pltpu.SemaphoreType.DMA((6,)),
            pltpu.SemaphoreType.DMA((50,)),
            pltpu.SemaphoreType.DMA((50,)),
        ],
        compiler_params=pltpu.CompilerParams(
            collective_id=0, has_side_effects=True, vmem_limit_bytes=56 * 1024 * 1024
        ),
        name="object_update",
    )(object_field, probe, amplitudes, dft_tables(), centers, live)
    return object_field + update.astype(f32)


def solution(mesh):
    return jax.shard_map(
        on_device,
        mesh=mesh,
        in_specs=(
            P(None, "tx", "ty"),
            P(None, "mode", None, None),
            P("tx", "ty", None, None, None),
            P("tx", "ty", None, None),
            P("tx", "ty"),
        ),
        out_specs=P(None, "tx", "ty"),
        check_vma=False,
    )
```

```python
import math

import jax
import jax.numpy as jnp
import numpy as np
from jax import lax
from jax.experimental import pallas as pl
from jax.experimental.pallas import tpu as pltpu
from jax.sharding import PartitionSpec as P

power_floor = 0.01
regularizer = 0.1
W = 256
HW = 128
TR = 128
TC = 256
Q = 32
f32 = jnp.float32
bf16 = jnp.bfloat16
i32 = jnp.int32
MESH = pl.DeviceIdType.MESH


def dft_tables():
    line = np.arange(W)
    angle = ((line[:, None] * line[None, :]) % W).astype(np.float32) * np.float32(2.0 * math.pi / W)
    scaling = np.float32(1.0 / math.sqrt(W))
    return jnp.asarray(
        np.stack([np.cos(angle) * scaling, -np.sin(angle) * scaling]).astype(np.float32)
    ).astype(bf16)


def dot(a, b):
    return jnp.dot(a, b, preferred_element_type=f32)


def one_hot(cond):
    return jnp.where(cond, 1.0, 0.0).astype(bf16)


def iota(shape, dim):
    return lax.broadcasted_iota(i32, shape, dim)


def kernel(
    obj_hbm,
    probe_hbm,
    amp_hbm,
    table_hbm,
    centers_hbm,
    live_hbm,
    out_ref,
    obj_v,
    probe_v,
    amp_v,
    tab,
    pb,
    pad,
    ib,
    mat_a,
    mat_b,
    mat_bc,
    mat_d,
    sel_p,
    sel_s,
    sel_pt,
    sel_st,
    patch,
    x_s,
    h_s,
    far_s,
    pow_s,
    wt,
    fix_s,
    r_s,
    back_s,
    grad,
    ext,
    zrecv,
    xsend,
    xrecv,
    mid,
    core_s,
    rs_s,
    rs_r,
    ag_s,
    wq,
    wt_low,
    sel_near,
    centers_ref,
    live_ref,
    local_sem,
    send,
    recv,
):
    tx, ty, m = lax.axis_index("tx"), lax.axis_index("ty"), lax.axis_index("mode")
    nx, ny, nm = lax.axis_size("tx"), lax.axis_size("ty"), lax.axis_size("mode")
    half_ny = ny // 2
    c = lax.rem(tx, 2)
    slot = m // 2
    part = lax.rem(m, 2)

    def at(tx_at, ty_at, m_at):
        return (tx_at, ty_at, m_at)

    right_ty = lax.rem(ty + 1, ny)
    left_ty = lax.rem(ty + ny - 1, ny)
    right_m = jnp.where(lax.rem(ty, half_ny) == half_ny - 1, nm - 1 - m, m)
    left_m = jnp.where(lax.rem(ty, half_ny) == 0, nm - 1 - m, m)
    right = at(tx, right_ty, right_m)
    left = at(tx, left_ty, left_m)
    up = at(lax.rem(tx + nx - 1, nx), ty, m)
    down = at(lax.rem(tx + 1, nx), ty, m)
    partner = at(tx + 1 - 2 * c, ty, m)
    far_ty = lax.rem(ty + half_ny, ny)
    ring_up = at(tx, jnp.where(m == nm - 1, far_ty, ty), lax.rem(m + 1, nm))
    ring_down = at(tx, jnp.where(m == 0, far_ty, ty), lax.rem(m + nm - 1, nm))
    mates = [at(tx, ty, lax.rem(m + d, nm)) for d in (1, 2, 3)]

    def remote(index, src, dst, to):
        return pltpu.make_async_remote_copy(
            src_ref=src,
            dst_ref=dst,
            send_sem=send.at[index],
            recv_sem=recv.at[index],
            device_id=to,
            device_id_type=MESH,
        )

    started = []

    def go(index, src, dst, to):
        copy = remote(index, src, dst, to)
        copy.start()
        started.append(copy)
        return copy

    loads = [
        pltpu.make_async_copy(obj_hbm, obj_v, local_sem.at[0]),
        pltpu.make_async_copy(probe_hbm, probe_v, local_sem.at[1]),
        pltpu.make_async_copy(table_hbm, tab, local_sem.at[2]),
        pltpu.make_async_copy(amp_hbm.at[0, 0], amp_v, local_sem.at[3]),
        pltpu.make_async_copy(centers_hbm, centers_ref, local_sem.at[4]),
        pltpu.make_async_copy(live_hbm, live_ref, local_sem.at[5]),
    ]
    for load in loads:
        load.start()

    barrier = pltpu.get_barrier_semaphore()
    meets = [left, right, up, down, ring_up, ring_down, *mates]
    for to in meets:
        pl.semaphore_signal(barrier, inc=1, device_id=to, device_id_type=MESH)

    loads[0].wait()
    for p in range(2):
        pad[p, HW : HW + TR, HW : HW + TC] = obj_v[p].astype(bf16)
    pl.semaphore_wait(barrier, len(meets))

    mid_rows = pl.ds(HW, TR)
    top_rows = pl.ds(0, HW)
    low_rows = pl.ds(HW + TR, HW)
    mid_cols = pl.ds(HW, TC)
    left_cols = pl.ds(0, HW)
    right_cols = pl.ds(HW + TC, HW)
    to_left, to_right = [], []
    for p in range(2):
        to_left.append(
            go(p, pad.at[p, mid_rows, pl.ds(HW, HW)], pad.at[p, mid_rows, right_cols], left)
        )
        to_right.append(
            go(44 + p, pad.at[p, mid_rows, pl.ds(TC, HW)], pad.at[p, mid_rows, left_cols], right)
        )
    z_up = go(4, pad.at[:, mid_rows, mid_cols], pad.at[:, low_rows, mid_cols], up)
    z_down = go(5, pad.at[:, mid_rows, mid_cols], pad.at[:, top_rows, mid_cols], down)

    loads[4].wait()
    loads[5].wait()
    row = iota((8, 128), 0)
    ints = jnp.zeros((8, 128), i32)
    for at_row, value in enumerate(
        [
            centers_ref[0, 0, 0, 0],
            centers_ref[0, 0, 0, 1],
            centers_ref[0, 0, 1, 0],
            centers_ref[0, 0, 1, 1],
            live_ref[0, 0],
        ]
    ):
        ints = jnp.where(row == at_row, value, ints)
    ib[1, 1] = ints

    ints_left = go(2, ib.at[1, 1], ib.at[1, 2], left)
    ints_right = go(3, ib.at[1, 1], ib.at[1, 0], right)

    loads[1].wait()
    for p in range(2):
        pb[0, 0, p] = probe_v[p, c].astype(bf16)
    ring = {}
    ring[3, 0] = go(12, pb.at[0, 0, 0], pb.at[3, 0, 0], ring_up)
    ring[1, 1] = go(13, pb.at[0, 0, 1], pb.at[1, 0, 1], ring_down)
    ring[3, 1] = go(14, pb.at[0, 0, 1], pb.at[3, 0, 1], ring_up)
    ring[1, 0] = go(15, pb.at[0, 0, 0], pb.at[1, 0, 0], ring_down)
    for p in range(2):
        pb[0, 1, p] = probe_v[p, 1 - c].astype(bf16)

    loads[2].wait()
    fr, fi = tab[0], tab[1]
    rows_here = pl.ds(pl.multiple_of(part * HW, HW), HW)
    fr_half, fi_half = tab[0, rows_here, :], tab[1, rows_here, :]
    mat_a[0:HW, 0:W] = fr_half
    mat_a[0:HW, W : 2 * W] = -fi_half
    mat_a[HW:W, 0:W] = fi_half
    mat_a[HW:W, W : 2 * W] = fr_half
    mat_b[0:W, 0:W] = fr
    mat_b[0:W, W : 2 * W] = fi
    mat_b[W : 2 * W, 0:W] = -fi
    mat_b[W : 2 * W, W : 2 * W] = fr
    mat_bc[0:W, 0:W] = fr
    mat_bc[0:W, W : 2 * W] = -fi
    mat_bc[W : 2 * W, 0:W] = fi
    mat_bc[W : 2 * W, W : 2 * W] = fr
    cols_here = pl.ds(pl.multiple_of(part * HW, HW), HW)
    fr_cols, fi_cols = tab[0, :, cols_here], tab[1, :, cols_here]
    mat_d[0:W, 0:HW] = fr_cols
    mat_d[0:W, HW:W] = fi_cols
    mat_d[W : 2 * W, 0:HW] = -fi_cols
    mat_d[W : 2 * W, HW:W] = fr_cols

    row_at = jnp.where(slot == 0, centers_ref[0, 0, 0, 0], centers_ref[0, 0, 1, 0])
    col_at = jnp.where(slot == 0, centers_ref[0, 0, 0, 1], centers_ref[0, 0, 1, 1])
    row_from = jnp.where(tx == 0, HW, 0)
    row_to = jnp.where(tx == nx - 1, HW + TR, TR + W)
    col_from = jnp.where(ty == 0, HW, 0)
    col_to = jnp.where(ty == ny - 1, HW + TC, TC + W)

    def selection(shape, outer, base, start, stop):
        big, small = iota(shape, outer), iota(shape, 1 - outer)
        return one_hot((big == small + base) & (big >= start) & (big < stop))

    sel_p[...] = selection((W, TR + W), 1, row_at, row_from, row_to)
    sel_pt[...] = selection((TR + W, W), 0, row_at, row_from, row_to)
    sel_s[...] = selection((TC + W, W), 0, col_at, col_from, col_to)
    sel_st[...] = selection((W, TC + W), 1, col_at, col_from, col_to)

    side = {}

    def pass_on(index, d, p):
        side[d, p] = go(index, pb.at[d, 0, p], pb.at[d, 1, p], partner)

    z_sides = []
    for p in range(2):
        to_left[p].wait_recv()
        to_right[p].wait_recv()
        for i, cols in enumerate((left_cols, right_cols)):
            here = pad.at[p, mid_rows, cols]
            z_sides.append(go(6 + 2 * p + i, here, pad.at[p, low_rows, cols], up))
            z_sides.append(go(46 + 2 * p + i, here, pad.at[p, top_rows, cols], down))
    ring[3, 0].wait_recv()
    ring[2, 0] = go(16, pb.at[3, 0, 0], pb.at[2, 0, 0], ring_up)
    ring[1, 1].wait_recv()
    ring[2, 1] = go(17, pb.at[1, 0, 1], pb.at[2, 0, 1], ring_down)
    pass_on(18, 3, 0)
    pass_on(19, 1, 1)

    ints_left.wait_recv()
    ints_right.wait_recv()
    ints_up = go(10, ib.at[1], ib.at[2], up)
    ints_down = go(11, ib.at[1], ib.at[0], down)

    ring[3, 1].wait_recv()
    pass_on(20, 3, 1)
    ring[1, 0].wait_recv()
    pass_on(21, 1, 0)

    chunk = 32
    for d, js in ((3, (0, 1)), (1, (1, 0))):
        for j in js:
            side[d, j].wait_recv()
    for i in range(W // chunk):
        at_rows = slice(i * chunk, (i + 1) * chunk)
        total = jnp.zeros((chunk, W), f32)
        for d in (0, 3, 1):
            for j in range(2):
                p_r = pb[d, j, 0, at_rows, :].astype(f32)
                p_i = pb[d, j, 1, at_rows, :].astype(f32)
                total = total + (p_r * p_r + p_i * p_i)
        wt[at_rows, :] = total
    z_up.wait_recv()
    z_down.wait_recv()
    for copy in z_sides:
        copy.wait_recv()
    for p in range(2):
        shifted = dot(sel_p[...], pad[p]).astype(bf16)
        patch[p] = dot(shifted, sel_s[...])

    ring[2, 0].wait_recv()
    pass_on(22, 2, 0)
    ring[2, 1].wait_recv()
    pass_on(23, 2, 1)

    def exits(d, buf, chunks, weigh=False):
        for i in chunks:
            at_rows, low_rows_at = slice(i * chunk, (i + 1) * chunk), slice(W + i * chunk, W + (i + 1) * chunk)
            o_r, o_i = patch[0, at_rows, :], patch[1, at_rows, :]
            for j in range(2):
                p_r = pb[d, j, 0, at_rows, :].astype(f32)
                p_i = pb[d, j, 1, at_rows, :].astype(f32)
                x_s[buf, j, at_rows, :] = (p_r * o_r - p_i * o_i).astype(bf16)
                x_s[buf, j, low_rows_at, :] = (p_r * o_i + p_i * o_r).astype(bf16)
                if weigh:
                    wt[at_rows, :] = wt[at_rows, :] + (p_r * p_r + p_i * p_i)

    def powers(d, first):
        for i in range(HW // chunk):
            at_rows = slice(i * chunk, (i + 1) * chunk)
            total = jnp.zeros((chunk, W), f32) if first else pow_s[at_rows, :]
            for j in range(2):
                rows = slice(j * HW + i * chunk, j * HW + (i + 1) * chunk)
                p, q = far_s[d, rows, 0:W], far_s[d, rows, W : 2 * W]
                total = total + (p * p + q * q)
            pow_s[at_rows, :] = total

    def forward(d, buf, then, weigh=False, last=None):
        for j in range(2):
            half = dot(mat_a[...], x_s[buf, j]).astype(bf16)
            h_s[j * HW : (j + 1) * HW, 0:W] = half[0:HW]
            h_s[j * HW : (j + 1) * HW, W : 2 * W] = half[HW:W]
            if then is not None:
                exits(then, 1 - buf, range(4 * j, 4 * j + 4), weigh)
        far_s[d] = dot(h_s[...], mat_b[...])
        if last is not None:
            powers(last, last == 0)

    exits(0, 0, range(8))
    forward(0, 0, 3)
    forward(3, 1, 1, last=0)
    side[2, 0].wait_recv()
    side[2, 1].wait_recv()
    forward(1, 0, 2, weigh=True, last=3)
    forward(2, 1, None, last=1)
    powers(2, False)

    loads[3].wait()
    amplitude = amp_v[slot, rows_here, :].astype(f32)
    pow_s[...] = amplitude / jnp.sqrt(pow_s[...] + power_floor)

    def fixes(d, buf):
        for i in range(HW // chunk):
            factor = pow_s[i * chunk : (i + 1) * chunk, :]
            for j in range(2):
                rows = slice(j * HW + i * chunk, j * HW + (i + 1) * chunk)
                fix_s[buf, rows, 0:W] = (far_s[d, rows, 0:W] * factor).astype(bf16)
                fix_s[buf, rows, W : 2 * W] = (far_s[d, rows, W : 2 * W] * factor).astype(bf16)

    def grads(d, buf, chunks):
        for i in chunks:
            at_rows, low_rows_at = slice(i * chunk, (i + 1) * chunk), slice(W + i * chunk, W + (i + 1) * chunk)
            g_r, g_i = grad[0, at_rows, :], grad[1, at_rows, :]
            for j in range(2):
                p_r = pb[d, j, 0, at_rows, :].astype(f32)
                p_i = pb[d, j, 1, at_rows, :].astype(f32)
                b_r, b_i = back_s[buf, j, at_rows, :], back_s[buf, j, low_rows_at, :]
                g_r = g_r + (p_r * b_r + p_i * b_i)
                g_i = g_i + (p_r * b_i - p_i * b_r)
            grad[0, at_rows, :] = g_r
            grad[1, at_rows, :] = g_i

    def backward(d, buf):
        half = dot(fix_s[buf], mat_bc[...]).astype(bf16)
        for j in range(2):
            r_s[j, 0:HW, :] = half[j * HW : (j + 1) * HW, 0:W]
            r_s[j, HW:W, :] = half[j * HW : (j + 1) * HW, W : 2 * W]
        if d < 3:
            fixes(d + 1, 1 - buf)
        for j in range(2):
            if d > 0:
                grads(d - 1, 1 - buf, range(4 * j, 4 * j + 4))
            back_s[buf, j] = dot(mat_d[...], r_s[j])

    for p in range(2):
        grad[p] = -0.5 * wt[...] * patch[p]
    fixes(0, 0)
    for d in range(4):
        backward(d, d % 2)
    grads(3, 1, range(8))

    counts = slot < live_ref[0, 0]
    folds = []
    for p in range(2):
        low = jnp.where(counts, grad[p], 0.0).astype(bf16)
        ext[p] = dot(sel_pt[...], low).astype(bf16)
        folds.append(
            (
                go(24 + 2 * p, ext.at[p, top_rows, :], zrecv.at[0, p], up),
                go(25 + 2 * p, ext.at[p, low_rows, :], zrecv.at[1, p], down),
            )
        )

    def weight_rows(a):
        total = jnp.zeros((Q, TC), f32) if a == 0 else wq[...]
        for b in range(3):
            inside = (
                jnp.where(tx + (a - 1) >= 0, 1, 0)
                * jnp.where(tx + (a - 1) < nx, 1, 0)
                * jnp.where(ty + (b - 1) >= 0, 1, 0)
                * jnp.where(ty + (b - 1) < ny, 1, 0)
            )
            block = ib[a, b]
            alive = block[4:5, 0:1] * inside
            for s in range(2):
                row_of = m * Q + HW - HW * (a - 1) - block[2 * s : 2 * s + 1, 0:1]
                col_of = HW - TC * (b - 1) - block[2 * s + 1 : 2 * s + 2, 0:1]
                pick = one_hot((iota((Q, W), 1) == iota((Q, W), 0) + row_of) & (alive > s))
                place = one_hot(iota((W, TC), 0) == iota((W, TC), 1) + col_of)
                picked = dot(pick, wt_low[...]).astype(bf16)
                total = total + dot(picked, place)
        wq[...] = total

    wt_low[...] = wt[...].astype(bf16)
    ints_up.wait_recv()
    ints_down.wait_recv()
    for index, a in ((0, 2), (1, 0)):
        block = ib[a, 1]
        col_there = jnp.where(slot == 0, block[1:2, 0:1], block[3:4, 0:1])
        sel_near[index] = selection((W, TC + W), 1, col_there, col_from, col_to)
    for p in range(2):
        mid[p] = dot(ext[p, HW : HW + TR, :], sel_st[...])

    columns = []
    for p in range(2):
        for copy in folds[p]:
            copy.wait_recv()
        mid[p] = mid[p] + (
            dot(zrecv[0, p], sel_near[0]) + dot(zrecv[1, p], sel_near[1])
        )
        xsend[p, 0] = mid[p, :, 0:HW].astype(bf16)
        xsend[p, 1] = mid[p, :, HW + TC :].astype(bf16)
        columns.append(
            (
                go(28 + 2 * p, xsend.at[p, 0], xrecv.at[p, 1], left),
                go(29 + 2 * p, xsend.at[p, 1], xrecv.at[p, 0], right),
            )
        )
    weight_rows(0)
    weight_rows(1)

    sums = []
    for p in range(2):
        for copy in columns[p]:
            copy.wait_recv()
        for q in range(4):
            rows = slice(q * Q, (q + 1) * Q)
            core_s[p, q, :, 0:HW] = mid[p, rows, HW : 2 * HW] + xrecv[p, 0, rows, :].astype(f32)
            core_s[p, q, :, HW:TC] = mid[p, rows, 2 * HW : 3 * HW] + xrecv[p, 1, rows, :].astype(f32)
            rs_s[p, q] = core_s[p, q].astype(bf16)
        sums.append(
            [
                go(31 + 3 * p + d, rs_s.at[p, lax.rem(m + d, nm)], rs_r.at[p, d - 1], mates[d - 1])
                for d in (1, 2, 3)
            ]
        )
    weight_rows(2)
    scale = wq[...] + regularizer

    gathers = []
    for p in range(2):
        total = core_s[p, m]
        for d in (1, 2, 3):
            sums[p][d - 1].wait_recv()
            total = total + rs_r[p, d - 1].astype(f32)
        ag_s[p, m] = (total / scale).astype(bf16)
        gathers.append(
            [go(37 + 3 * p + d, ag_s.at[p, m], ag_s.at[p, m], mates[d - 1]) for d in (1, 2, 3)]
        )
    for p in range(2):
        for copy in gathers[p]:
            copy.wait_recv()
        for q in range(4):
            out_ref[p, q * Q : (q + 1) * Q, :] = ag_s[p, q]
    for copy in started:
        copy.wait_send()


def on_device(object_field, probe, amplitudes, centers, live):
    any_space = pl.BlockSpec(memory_space=pl.ANY)
    vmem = pltpu.VMEM
    update = pl.pallas_call(
        kernel,
        out_shape=pltpu.VMEM((2, TR, TC), bf16),
        in_specs=[any_space] * 6,
        out_specs=pl.BlockSpec(memory_space=pltpu.VMEM),
        scratch_shapes=[
            vmem((2, TR, TC), f32),
            vmem((2, 2, W, W), f32),
            vmem((2, W, W), bf16),
            vmem((2, W, W), bf16),
            vmem((4, 2, 2, W, W), bf16),
            vmem((2, TR + W, TC + W), bf16),
            vmem((3, 3, 8, 128), i32),
            vmem((W, 2 * W), bf16),
            vmem((2 * W, 2 * W), bf16),
            vmem((2 * W, 2 * W), bf16),
            vmem((2 * W, W), bf16),
            vmem((W, TR + W), bf16),
            vmem((TC + W, W), bf16),
            vmem((TR + W, W), bf16),
            vmem((W, TC + W), bf16),
            vmem((2, W, W), f32),
            vmem((2, 2, 2 * W, W), bf16),
            vmem((W, 2 * W), bf16),
            vmem((4, W, 2 * W), f32),
            vmem((HW, W), f32),
            vmem((W, W), f32),
            vmem((2, W, 2 * W), bf16),
            vmem((2, W, W), bf16),
            vmem((2, 2, 2 * W, W), f32),
            vmem((2, W, W), f32),
            vmem((2, TR + W, W), bf16),
            vmem((2, 2, HW, W), bf16),
            vmem((2, 2, TR, HW), bf16),
            vmem((2, 2, TR, HW), bf16),
            vmem((2, TR, TC + W), f32),
            vmem((2, 4, Q, TC), f32),
            vmem((2, 4, Q, TC), bf16),
            vmem((2, 3, Q, TC), bf16),
            vmem((2, 4, Q, TC), bf16),
            vmem((Q, TC), f32),
            vmem((W, W), bf16),
            vmem((2, W, TC + W), bf16),
            pltpu.SMEM((1, 1, 2, 2), i32),
            pltpu.SMEM((1, 1), i32),
            pltpu.SemaphoreType.DMA((6,)),
            pltpu.SemaphoreType.DMA((50,)),
            pltpu.SemaphoreType.DMA((50,)),
        ],
        compiler_params=pltpu.CompilerParams(
            collective_id=0, has_side_effects=True, vmem_limit_bytes=56 * 1024 * 1024
        ),
        name="object_update",
    )(object_field, probe, amplitudes, dft_tables(), centers, live)
    return object_field + update.astype(f32)


def solution(mesh):
    return jax.shard_map(
        on_device,
        mesh=mesh,
        in_specs=(
            P(None, "tx", "ty"),
            P(None, "mode", None, None),
            P("tx", "ty", None, None, None),
            P("tx", "ty", None, None),
            P("tx", "ty"),
        ),
        out_specs=P(None, "tx", "ty"),
        check_vma=False,
    )
```

```python
import math

import jax
import jax.numpy as jnp
import numpy as np
from jax import lax
from jax.experimental import pallas as pl
from jax.experimental.pallas import tpu as pltpu
from jax.sharding import PartitionSpec as P

power_floor = 0.01
regularizer = 0.1
W = 256
HW = 128
TR = 128
TC = 256
Q = 32
f32 = jnp.float32
bf16 = jnp.bfloat16
i32 = jnp.int32
MESH = pl.DeviceIdType.MESH


def dft_tables():
    line = np.arange(W)
    angle = ((line[:, None] * line[None, :]) % W).astype(np.float32) * np.float32(2.0 * math.pi / W)
    scaling = np.float32(1.0 / math.sqrt(W))
    return jnp.asarray(
        np.stack([np.cos(angle) * scaling, -np.sin(angle) * scaling]).astype(np.float32)
    ).astype(bf16)


def dot(a, b):
    return jnp.dot(a, b, preferred_element_type=f32)


def one_hot(cond):
    return jnp.where(cond, 1.0, 0.0).astype(bf16)


def iota(shape, dim):
    return lax.broadcasted_iota(i32, shape, dim)


def kernel(
    obj_hbm,
    probe_hbm,
    amp_hbm,
    table_hbm,
    centers_hbm,
    live_hbm,
    out_ref,
    obj_v,
    probe_v,
    amp_v,
    tab,
    pb,
    pad,
    ib,
    mat_a,
    mat_b,
    mat_bc,
    mat_d,
    sel_p,
    sel_s,
    sel_pt,
    sel_st,
    patch,
    x_s,
    h_s,
    far_s,
    pow_s,
    wt,
    fix_s,
    r_s,
    back_s,
    grad,
    ext,
    zrecv,
    xsend,
    xrecv,
    mid,
    core_s,
    rs_s,
    rs_r,
    ag_s,
    wq,
    wt_low,
    sel_near,
    cols_s,
    centers_ref,
    live_ref,
    local_sem,
    send,
    recv,
):
    tx, ty, m = lax.axis_index("tx"), lax.axis_index("ty"), lax.axis_index("mode")
    nx, ny, nm = lax.axis_size("tx"), lax.axis_size("ty"), lax.axis_size("mode")
    half_ny = ny // 2
    c = lax.rem(tx, 2)
    slot = m // 2
    part = lax.rem(m, 2)

    def at(tx_at, ty_at, m_at):
        return (tx_at, ty_at, m_at)

    right_ty = lax.rem(ty + 1, ny)
    left_ty = lax.rem(ty + ny - 1, ny)
    right_m = jnp.where(lax.rem(ty, half_ny) == half_ny - 1, nm - 1 - m, m)
    left_m = jnp.where(lax.rem(ty, half_ny) == 0, nm - 1 - m, m)
    right = at(tx, right_ty, right_m)
    left = at(tx, left_ty, left_m)
    up = at(lax.rem(tx + nx - 1, nx), ty, m)
    down = at(lax.rem(tx + 1, nx), ty, m)
    partner = at(tx + 1 - 2 * c, ty, m)
    far_ty = lax.rem(ty + half_ny, ny)
    ring_up = at(tx, jnp.where(m == nm - 1, far_ty, ty), lax.rem(m + 1, nm))
    ring_down = at(tx, jnp.where(m == 0, far_ty, ty), lax.rem(m + nm - 1, nm))
    mates = [at(tx, ty, lax.rem(m + d, nm)) for d in (1, 2, 3)]

    def remote(index, src, dst, to):
        return pltpu.make_async_remote_copy(
            src_ref=src,
            dst_ref=dst,
            send_sem=send.at[index],
            recv_sem=recv.at[index],
            device_id=to,
            device_id_type=MESH,
        )

    started = []

    def go(index, src, dst, to):
        copy = remote(index, src, dst, to)
        copy.start()
        started.append(copy)
        return copy

    loads = [
        pltpu.make_async_copy(obj_hbm, obj_v, local_sem.at[0]),
        pltpu.make_async_copy(probe_hbm, probe_v, local_sem.at[1]),
        pltpu.make_async_copy(table_hbm, tab, local_sem.at[2]),
        pltpu.make_async_copy(amp_hbm.at[0, 0], amp_v, local_sem.at[3]),
        pltpu.make_async_copy(centers_hbm, centers_ref, local_sem.at[4]),
        pltpu.make_async_copy(live_hbm, live_ref, local_sem.at[5]),
    ]
    for load in loads:
        load.start()

    barrier = pltpu.get_barrier_semaphore()
    meets = [left, right, up, down, ring_up, ring_down, *mates]
    for to in meets:
        pl.semaphore_signal(barrier, inc=1, device_id=to, device_id_type=MESH)

    loads[0].wait()
    for p in range(2):
        pad[p, HW : HW + TR, HW : HW + TC] = obj_v[p].astype(bf16)
    pl.semaphore_wait(barrier, len(meets))

    mid_rows = pl.ds(HW, TR)
    top_rows = pl.ds(0, HW)
    low_rows = pl.ds(HW + TR, HW)
    mid_cols = pl.ds(HW, TC)
    left_cols = pl.ds(0, HW)
    right_cols = pl.ds(HW + TC, HW)
    to_left, to_right = [], []
    for p in range(2):
        to_left.append(
            go(p, pad.at[p, mid_rows, pl.ds(HW, HW)], pad.at[p, mid_rows, right_cols], left)
        )
        to_right.append(
            go(44 + p, pad.at[p, mid_rows, pl.ds(TC, HW)], pad.at[p, mid_rows, left_cols], right)
        )
    z_up = go(4, pad.at[:, mid_rows, mid_cols], pad.at[:, low_rows, mid_cols], up)
    z_down = go(5, pad.at[:, mid_rows, mid_cols], pad.at[:, top_rows, mid_cols], down)

    loads[4].wait()
    loads[5].wait()
    row = iota((8, 128), 0)
    ints = jnp.zeros((8, 128), i32)
    for at_row, value in enumerate(
        [
            centers_ref[0, 0, 0, 0],
            centers_ref[0, 0, 0, 1],
            centers_ref[0, 0, 1, 0],
            centers_ref[0, 0, 1, 1],
            live_ref[0, 0],
        ]
    ):
        ints = jnp.where(row == at_row, value, ints)
    ib[1, 1] = ints

    ints_left = go(2, ib.at[1, 1], ib.at[1, 2], left)
    ints_right = go(3, ib.at[1, 1], ib.at[1, 0], right)

    loads[1].wait()
    for p in range(2):
        pb[0, 0, p] = probe_v[p, c].astype(bf16)
    ring = {}
    ring[3, 0] = go(12, pb.at[0, 0, 0], pb.at[3, 0, 0], ring_up)
    ring[1, 1] = go(13, pb.at[0, 0, 1], pb.at[1, 0, 1], ring_down)
    ring[3, 1] = go(14, pb.at[0, 0, 1], pb.at[3, 0, 1], ring_up)
    ring[1, 0] = go(15, pb.at[0, 0, 0], pb.at[1, 0, 0], ring_down)
    for p in range(2):
        pb[0, 1, p] = probe_v[p, 1 - c].astype(bf16)

    loads[2].wait()
    fr, fi = tab[0], tab[1]
    rows_here = pl.ds(pl.multiple_of(part * HW, HW), HW)
    fr_half, fi_half = tab[0, rows_here, :], tab[1, rows_here, :]
    mat_a[0:HW, 0:W] = fr_half
    mat_a[0:HW, W : 2 * W] = -fi_half
    mat_a[HW:W, 0:W] = fi_half
    mat_a[HW:W, W : 2 * W] = fr_half
    mat_b[0:W, 0:W] = fr
    mat_b[0:W, W : 2 * W] = fi
    mat_b[W : 2 * W, 0:W] = -fi
    mat_b[W : 2 * W, W : 2 * W] = fr
    mat_bc[0:W, 0:W] = fr
    mat_bc[0:W, W : 2 * W] = -fi
    mat_bc[W : 2 * W, 0:W] = fi
    mat_bc[W : 2 * W, W : 2 * W] = fr
    cols_here = pl.ds(pl.multiple_of(part * HW, HW), HW)
    fr_cols, fi_cols = tab[0, :, cols_here], tab[1, :, cols_here]
    mat_d[0:W, 0:HW] = fr_cols
    mat_d[0:W, HW:W] = fi_cols
    mat_d[W : 2 * W, 0:HW] = -fi_cols
    mat_d[W : 2 * W, HW:W] = fr_cols

    row_at = jnp.where(slot == 0, centers_ref[0, 0, 0, 0], centers_ref[0, 0, 1, 0])
    col_at = jnp.where(slot == 0, centers_ref[0, 0, 0, 1], centers_ref[0, 0, 1, 1])
    row_from = jnp.where(tx == 0, HW, 0)
    row_to = jnp.where(tx == nx - 1, HW + TR, TR + W)
    col_from = jnp.where(ty == 0, HW, 0)
    col_to = jnp.where(ty == ny - 1, HW + TC, TC + W)

    def selection(shape, outer, base, start, stop):
        big, small = iota(shape, outer), iota(shape, 1 - outer)
        return one_hot((big == small + base) & (big >= start) & (big < stop))

    sel_p[...] = selection((W, TR + W), 1, row_at, row_from, row_to)
    sel_pt[...] = selection((TR + W, W), 0, row_at, row_from, row_to)
    sel_s[...] = selection((TC + W, W), 0, col_at, col_from, col_to)
    sel_st[...] = selection((W, TC + W), 1, col_at, col_from, col_to)

    side = {}

    def pass_on(index, d, p):
        side[d, p] = go(index, pb.at[d, 0, p], pb.at[d, 1, p], partner)

    ring[3, 0].wait_recv()
    ring[2, 0] = go(16, pb.at[3, 0, 0], pb.at[2, 0, 0], ring_up)
    ring[1, 1].wait_recv()
    ring[2, 1] = go(17, pb.at[1, 0, 1], pb.at[2, 0, 1], ring_down)
    z_sides = []
    for p in range(2):
        to_left[p].wait_recv()
        to_right[p].wait_recv()
        for i, cols in enumerate((left_cols, right_cols)):
            here = pad.at[p, mid_rows, cols]
            z_sides.append(go(6 + 2 * p + i, here, pad.at[p, low_rows, cols], up))
            z_sides.append(go(46 + 2 * p + i, here, pad.at[p, top_rows, cols], down))
    pass_on(18, 3, 0)
    pass_on(19, 1, 1)

    ints_left.wait_recv()
    ints_right.wait_recv()
    ints_up = go(10, ib.at[1], ib.at[2], up)
    ints_down = go(11, ib.at[1], ib.at[0], down)

    ring[3, 1].wait_recv()
    pass_on(20, 3, 1)
    ring[1, 0].wait_recv()
    pass_on(21, 1, 0)

    chunk = 32
    for i in range(W // chunk):
        at_rows = slice(i * chunk, (i + 1) * chunk)
        total = jnp.zeros((chunk, W), f32)
        for d in (0,):
            for j in range(2):
                p_r = pb[d, j, 0, at_rows, :].astype(f32)
                p_i = pb[d, j, 1, at_rows, :].astype(f32)
                total = total + (p_r * p_r + p_i * p_i)
        wt[at_rows, :] = total
    for p in range(2):
        cols_s[p, HW : HW + TR, :] = dot(pad[p, HW : HW + TR, :], sel_s[...]).astype(bf16)
    z_up.wait_recv()
    z_down.wait_recv()
    for copy in z_sides:
        copy.wait_recv()
    for p in range(2):
        for rows in (slice(0, HW), slice(HW + TR, TR + W)):
            cols_s[p, rows, :] = dot(pad[p, rows, :], sel_s[...]).astype(bf16)
        patch[p] = dot(sel_p[...], cols_s[p])

    ring[2, 0].wait_recv()
    pass_on(22, 2, 0)
    ring[2, 1].wait_recv()
    pass_on(23, 2, 1)

    def exits(d, buf, chunks, weigh=False):
        for i in chunks:
            at_rows, low_rows_at = slice(i * chunk, (i + 1) * chunk), slice(W + i * chunk, W + (i + 1) * chunk)
            o_r, o_i = patch[0, at_rows, :], patch[1, at_rows, :]
            for j in range(2):
                p_r = pb[d, j, 0, at_rows, :].astype(f32)
                p_i = pb[d, j, 1, at_rows, :].astype(f32)
                x_s[buf, j, at_rows, :] = (p_r * o_r - p_i * o_i).astype(bf16)
                x_s[buf, j, low_rows_at, :] = (p_r * o_i + p_i * o_r).astype(bf16)
                if weigh:
                    wt[at_rows, :] = wt[at_rows, :] + (p_r * p_r + p_i * p_i)

    def powers(d, first):
        for i in range(HW // chunk):
            at_rows = slice(i * chunk, (i + 1) * chunk)
            total = jnp.zeros((chunk, W), f32) if first else pow_s[at_rows, :]
            for j in range(2):
                rows = slice(j * HW + i * chunk, j * HW + (i + 1) * chunk)
                p, q = far_s[d, rows, 0:W], far_s[d, rows, W : 2 * W]
                total = total + (p * p + q * q)
            pow_s[at_rows, :] = total

    def forward(d, buf, then, weigh=False, last=None):
        for j in range(2):
            half = dot(mat_a[...], x_s[buf, j]).astype(bf16)
            h_s[j * HW : (j + 1) * HW, 0:W] = half[0:HW]
            h_s[j * HW : (j + 1) * HW, W : 2 * W] = half[HW:W]
            if then is not None:
                exits(then, 1 - buf, range(4 * j, 4 * j + 4), weigh)
        far_s[d] = dot(h_s[...], mat_b[...])
        if last is not None:
            powers(last, last == 0)

    exits(0, 0, range(8))
    side[3, 0].wait_recv()
    side[3, 1].wait_recv()
    forward(0, 0, 3, weigh=True)
    side[1, 1].wait_recv()
    side[1, 0].wait_recv()
    forward(3, 1, 1, weigh=True, last=0)
    side[2, 0].wait_recv()
    side[2, 1].wait_recv()
    forward(1, 0, 2, weigh=True, last=3)
    forward(2, 1, None, last=1)
    powers(2, False)

    loads[3].wait()
    amplitude = amp_v[slot, rows_here, :].astype(f32)
    pow_s[...] = amplitude / jnp.sqrt(pow_s[...] + power_floor)

    def fixes(d, buf):
        for i in range(HW // chunk):
            factor = pow_s[i * chunk : (i + 1) * chunk, :]
            for j in range(2):
                rows = slice(j * HW + i * chunk, j * HW + (i + 1) * chunk)
                fix_s[buf, rows, 0:W] = (far_s[d, rows, 0:W] * factor).astype(bf16)
                fix_s[buf, rows, W : 2 * W] = (far_s[d, rows, W : 2 * W] * factor).astype(bf16)

    def grads(d, buf, chunks):
        for i in chunks:
            at_rows, low_rows_at = slice(i * chunk, (i + 1) * chunk), slice(W + i * chunk, W + (i + 1) * chunk)
            g_r, g_i = grad[0, at_rows, :], grad[1, at_rows, :]
            for j in range(2):
                p_r = pb[d, j, 0, at_rows, :].astype(f32)
                p_i = pb[d, j, 1, at_rows, :].astype(f32)
                b_r, b_i = back_s[buf, j, at_rows, :], back_s[buf, j, low_rows_at, :]
                g_r = g_r + (p_r * b_r + p_i * b_i)
                g_i = g_i + (p_r * b_i - p_i * b_r)
            grad[0, at_rows, :] = g_r
            grad[1, at_rows, :] = g_i

    def backward(d, buf):
        half = dot(fix_s[buf], mat_bc[...]).astype(bf16)
        for j in range(2):
            r_s[j, 0:HW, :] = half[j * HW : (j + 1) * HW, 0:W]
            r_s[j, HW:W, :] = half[j * HW : (j + 1) * HW, W : 2 * W]
        if d < 3:
            fixes(d + 1, 1 - buf)
        for j in range(2):
            if d > 0:
                grads(d - 1, 1 - buf, range(4 * j, 4 * j + 4))
            back_s[buf, j] = dot(mat_d[...], r_s[j])

    for p in range(2):
        grad[p] = -0.5 * wt[...] * patch[p]
    fixes(0, 0)
    for d in range(4):
        backward(d, d % 2)
    grads(3, 1, range(8))

    counts = slot < live_ref[0, 0]
    folds = []
    for p in range(2):
        low = jnp.where(counts, grad[p], 0.0).astype(bf16)
        ext[p] = dot(sel_pt[...], low).astype(bf16)
        folds.append(
            (
                go(24 + 2 * p, ext.at[p, top_rows, :], zrecv.at[0, p], up),
                go(25 + 2 * p, ext.at[p, low_rows, :], zrecv.at[1, p], down),
            )
        )

    def weight_rows(a):
        total = jnp.zeros((Q, TC), f32) if a == 0 else wq[...]
        for b in range(3):
            inside = (
                jnp.where(tx + (a - 1) >= 0, 1, 0)
                * jnp.where(tx + (a - 1) < nx, 1, 0)
                * jnp.where(ty + (b - 1) >= 0, 1, 0)
                * jnp.where(ty + (b - 1) < ny, 1, 0)
            )
            block = ib[a, b]
            alive = block[4:5, 0:1] * inside
            for s in range(2):
                row_of = m * Q + HW - HW * (a - 1) - block[2 * s : 2 * s + 1, 0:1]
                col_of = HW - TC * (b - 1) - block[2 * s + 1 : 2 * s + 2, 0:1]
                pick = one_hot((iota((Q, W), 1) == iota((Q, W), 0) + row_of) & (alive > s))
                place = one_hot(iota((W, TC), 0) == iota((W, TC), 1) + col_of)
                picked = dot(pick, wt_low[...]).astype(bf16)
                total = total + dot(picked, place)
        wq[...] = total

    wt_low[...] = wt[...].astype(bf16)
    ints_up.wait_recv()
    ints_down.wait_recv()
    for index, a in ((0, 2), (1, 0)):
        block = ib[a, 1]
        col_there = jnp.where(slot == 0, block[1:2, 0:1], block[3:4, 0:1])
        sel_near[index] = selection((W, TC + W), 1, col_there, col_from, col_to)
    for p in range(2):
        mid[p] = dot(ext[p, HW : HW + TR, :], sel_st[...])

    columns = []
    for p in range(2):
        for copy in folds[p]:
            copy.wait_recv()
        mid[p] = mid[p] + (
            dot(zrecv[0, p], sel_near[0]) + dot(zrecv[1, p], sel_near[1])
        )
        xsend[p, 0] = mid[p, :, 0:HW].astype(bf16)
        xsend[p, 1] = mid[p, :, HW + TC :].astype(bf16)
        columns.append(
            (
                go(28 + 2 * p, xsend.at[p, 0], xrecv.at[p, 1], left),
                go(29 + 2 * p, xsend.at[p, 1], xrecv.at[p, 0], right),
            )
        )
    weight_rows(0)
    weight_rows(1)

    sums = []
    for p in range(2):
        for copy in columns[p]:
            copy.wait_recv()
        for q in range(4):
            rows = slice(q * Q, (q + 1) * Q)
            core_s[p, q, :, 0:HW] = mid[p, rows, HW : 2 * HW] + xrecv[p, 0, rows, :].astype(f32)
            core_s[p, q, :, HW:TC] = mid[p, rows, 2 * HW : 3 * HW] + xrecv[p, 1, rows, :].astype(f32)
            rs_s[p, q] = core_s[p, q].astype(bf16)
        sums.append(
            [
                go(31 + 3 * p + d, rs_s.at[p, lax.rem(m + d, nm)], rs_r.at[p, d - 1], mates[d - 1])
                for d in (1, 2, 3)
            ]
        )
    weight_rows(2)
    scale = wq[...] + regularizer

    gathers = []
    for p in range(2):
        total = core_s[p, m]
        for d in (1, 2, 3):
            sums[p][d - 1].wait_recv()
            total = total + rs_r[p, d - 1].astype(f32)
        ag_s[p, m] = (total / scale).astype(bf16)
        gathers.append(
            [go(37 + 3 * p + d, ag_s.at[p, m], ag_s.at[p, m], mates[d - 1]) for d in (1, 2, 3)]
        )
    for p in range(2):
        for copy in gathers[p]:
            copy.wait_recv()
        for q in range(4):
            out_ref[p, q * Q : (q + 1) * Q, :] = ag_s[p, q]
    for copy in started:
        copy.wait_send()


def on_device(object_field, probe, amplitudes, centers, live):
    any_space = pl.BlockSpec(memory_space=pl.ANY)
    vmem = pltpu.VMEM
    update = pl.pallas_call(
        kernel,
        out_shape=pltpu.VMEM((2, TR, TC), bf16),
        in_specs=[any_space] * 6,
        out_specs=pl.BlockSpec(memory_space=pltpu.VMEM),
        scratch_shapes=[
            vmem((2, TR, TC), f32),
            vmem((2, 2, W, W), f32),
            vmem((2, W, W), bf16),
            vmem((2, W, W), bf16),
            vmem((4, 2, 2, W, W), bf16),
            vmem((2, TR + W, TC + W), bf16),
            vmem((3, 3, 8, 128), i32),
            vmem((W, 2 * W), bf16),
            vmem((2 * W, 2 * W), bf16),
            vmem((2 * W, 2 * W), bf16),
            vmem((2 * W, W), bf16),
            vmem((W, TR + W), bf16),
            vmem((TC + W, W), bf16),
            vmem((TR + W, W), bf16),
            vmem((W, TC + W), bf16),
            vmem((2, W, W), f32),
            vmem((2, 2, 2 * W, W), bf16),
            vmem((W, 2 * W), bf16),
            vmem((4, W, 2 * W), f32),
            vmem((HW, W), f32),
            vmem((W, W), f32),
            vmem((2, W, 2 * W), bf16),
            vmem((2, W, W), bf16),
            vmem((2, 2, 2 * W, W), f32),
            vmem((2, W, W), f32),
            vmem((2, TR + W, W), bf16),
            vmem((2, 2, HW, W), bf16),
            vmem((2, 2, TR, HW), bf16),
            vmem((2, 2, TR, HW), bf16),
            vmem((2, TR, TC + W), f32),
            vmem((2, 4, Q, TC), f32),
            vmem((2, 4, Q, TC), bf16),
            vmem((2, 3, Q, TC), bf16),
            vmem((2, 4, Q, TC), bf16),
            vmem((Q, TC), f32),
            vmem((W, W), bf16),
            vmem((2, W, TC + W), bf16),
            vmem((2, TR + W, W), bf16),
            pltpu.SMEM((1, 1, 2, 2), i32),
            pltpu.SMEM((1, 1), i32),
            pltpu.SemaphoreType.DMA((6,)),
            pltpu.SemaphoreType.DMA((50,)),
            pltpu.SemaphoreType.DMA((50,)),
        ],
        compiler_params=pltpu.CompilerParams(
            collective_id=0, has_side_effects=True, vmem_limit_bytes=56 * 1024 * 1024
        ),
        name="object_update",
    )(object_field, probe, amplitudes, dft_tables(), centers, live)
    return object_field + update.astype(f32)


def solution(mesh):
    return jax.shard_map(
        on_device,
        mesh=mesh,
        in_specs=(
            P(None, "tx", "ty"),
            P(None, "mode", None, None),
            P("tx", "ty", None, None, None),
            P("tx", "ty", None, None),
            P("tx", "ty"),
        ),
        out_specs=P(None, "tx", "ty"),
        check_vma=False,
    )
```
